32 devices in a mesh: leaf: 8 (over z, core), front: 4 (over y, x).
Axes of the slice: x: 2, y: 2, z: 4, core: 2. Of those that a mesh axis runs over, the one named last changes fastest.
Arguments:
- blocks: bfloat16 [256, 128, 1024], P(('leaf', 'front')), may hold values from -0.1875 to 0.1875
- pattern: int32 [256, 8], P(('leaf', 'front')), may hold values 0 or 1
- assign: int32 [256, 1], P(('leaf', 'front')), may hold values from 0 to 7; in each aligned block of 8 rows (0 to 7, 8 to 15, ...) at most 2 rows name the same one
- order: int32 [8], replicated, may hold values from 0 to 7, each once
- leaf_map: int32 [8, 4], replicated, may hold values from 0 to 7, as said below
- mid_map: int32 [4, 4], replicated, may hold values from 0 to 7, as said below
- prior: float32 [8, 3, 1024], P('leaf'), may hold values from 1 to 4
Outputs:
- leaf_factor: float32 [8, 512, 1024], P('leaf', 'front')
- mid_factor: float32 [8, 256, 1024], P('leaf', 'front')
- top_factor: float32 [8, 256, 1024], P('leaf', 'front')
The draws below stay inside these ranges and needn't reach their ends.
Inputs may be any that keep to these rules, and one draw needn't show every extreme that they name: `assign`: in each aligned block of 8 rows (the row blocks of one device) no front is named more than 2 times; in every draw some block names some front exactly 2 times, and every front is named somewhere. `leaf_map`: each row holds 4 distinct numbers; rows 2k and 2k+1 share exactly 2 numbers. `mid_map`: each row holds 4 distinct numbers; rows 2k and 2k+1 share exactly 2 numbers.
All inputs are finite; a program needn't handle non-finite values. No bound on the sum of `pattern` on one device may be relied on, other than what follows from the above.
Results may differ from the reference program's by a relative error of at most 0.0003.
Values may be sent and summed in bfloat16 or wider, within the bound.
A program may use at most 128 MiB of HBM per device.

```python
import math
import jax
import jax.numpy as jnp
import numpy as np
from jax import lax

CB = 8
BLK = 128
W = 1024
RB = 8
CAP = 2
LEAVES = 8
BLOCKS = 256


def pair_maps(key, pairs):
    keys = jax.random.split(key, pairs)
    perms = jax.vmap(lambda single: jax.random.permutation(single, CB))(keys)
    first = perms[:, :CB // 2]
    second = perms[:, CB // 4:CB // 4 + CB // 2]
    return jnp.stack([first, second], 1).reshape(pairs * 2, CB // 2).astype(jnp.int32)


def draw_leaf_map(key, part):
    return pair_maps(jax.random.fold_in(key, 11), LEAVES // 2)


def draw_mid_map(key, part):
    return pair_maps(jax.random.fold_in(key, 13), LEAVES // 4)


def set_ends(drawn, stream_key, least, top_value):
    shape = drawn.shape
    place = [jax.random.randint(jax.random.fold_in(stream_key, axis), (), 0, shape[axis]) for axis in range(len(shape))]
    drawn = drawn.at[tuple(place)].set(least)
    longest = shape.index(max(shape))
    place[longest] = (place[longest] + 1) % shape[longest]
    return drawn.at[tuple(place)].set(top_value)


def steps_of(key, dims, shards, least, high):
    def one(position, parts):
        steps = jax.random.uniform(jax.random.fold_in(jax.random.fold_in(key, 6), position), (parts,), jnp.float32, least / len(shards), high / len(shards))
        return jnp.repeat(jnp.exp(steps), dims[position] // parts).reshape((-1,) + (1,) * (len(dims) - position - 1))

    gain = one(*shards[0])
    for cut in shards[1:]:
        gain = gain * one(*cut)
    return gain


def deal_out(own_key, own, number, rows, amount, top, most, slope):
    ranking = jax.random.permutation(own_key, amount)
    heavy_load, ordinary = load_shares(amount, rows * top, most, slope, True), load_shares(amount, rows * top, most, slope, False)
    places = jnp.arange(amount)

    def named(lengths, turn):
        used = int((lengths > 0).sum())
        fixed = max(1, used // 4)
        moved = fixed + (places - fixed + turn * (used - fixed)) % max(1, amount - fixed)
        return jnp.zeros((amount,), jnp.int32).at[ranking[jnp.where(places < fixed, places, moved)]].set(jnp.asarray(lengths, jnp.int32))

    lengths = jnp.where(number % 4 == 0, named(heavy_load, number // 4), named(ordinary, number - number // 4 - 1))
    mixed = jax.random.permutation(jax.random.fold_in(own, 3), amount)
    giver, sink = mixed[0:amount // 2 * 2:2], mixed[1:amount // 2 * 2:2]
    slack = jnp.minimum(lengths[giver] - 1, most - lengths[sink]) // 2
    slack = jnp.where((giver == ranking[0]) | (sink == ranking[0]) | (lengths[sink] == 0), 0, jnp.maximum(slack, 0))
    moved = jax.random.randint(jax.random.fold_in(own, 4), (amount // 2,), 0, 1 << 20) % (slack + 1)
    lengths = lengths.at[giver].add(-moved).at[sink].add(moved)
    items = jnp.searchsorted(jnp.cumsum(lengths), jnp.arange(rows * top), side="right").astype(jnp.int32)
    listing = items.reshape(top, rows).T
    listing = listing[jax.random.permutation(jax.random.fold_in(own, 1), rows)]
    turn = jax.random.randint(jax.random.fold_in(own, 2), (rows, 1), 0, top)
    return jnp.take_along_axis(listing, (jnp.arange(top)[None, :] + turn) % top, axis=1)


def load_shares(amount, total, limit, skew, full):
    portions = [(1 << 20) // math.isqrt(standing ** skew) + 1 for standing in range(1, amount + 1)]
    largest = limit if full else min(limit, max(-(-total // amount), total * portions[0] // sum(portions)))
    least = 1 if total - largest >= amount - 1 else 0
    given, rest = [largest] + [least] * (amount - 1), total - largest - least * (amount - 1)
    while rest > 0:
        free = [i for i in range(1, amount) if given[i] < largest] or [i for i in range(1, amount) if given[i] < limit]
        whole, budget = sum([portions[i] for i in free]), rest
        for i in free:
            extra = min(limit - given[i], max(1, budget * portions[i] // whole), rest)
            given[i] = given[i] + extra
            rest = rest - extra
    return np.array(given)


def scatter_about(stream_key, extent, deviation, limit, cuts=(), held_as=jnp.bfloat16):
    array = jax.random.normal(stream_key, extent, jnp.float32) * deviation
    if len(cuts) > 0:
        array = steps_of(stream_key, extent, cuts, -0.22, 0.18) * array
    return jnp.clip(array, min=-limit, max=limit).astype(held_as)


def setup_inputs(seed: int = 0) -> dict:
    streams_of = jax.random.split(jax.random.key(seed), 8)
    blocks = scatter_about(streams_of[0], (BLOCKS, BLK, W), (RB * BLK) ** -0.5, 0.1875, ((0, 32),))
    pattern = set_ends((jax.random.randint(streams_of[1], (BLOCKS, CB), 0, 4) < 3).astype(jnp.int32), jax.random.fold_in(streams_of[1], 1), 0, 1)
    assign_keys = jax.random.split(jax.random.fold_in(streams_of[2], 1), BLOCKS // RB)
    assign_turns = jax.random.permutation(jax.random.fold_in(streams_of[2], 3), BLOCKS // RB)
    assign = jax.vmap(lambda own, number: deal_out(jax.random.fold_in(streams_of[2], 2), own, number, RB, LEAVES, 1, CAP, 2))(assign_keys, assign_turns).reshape((BLOCKS, 1))
    order = jax.random.permutation(streams_of[3], LEAVES).astype(jnp.int32)
    leaf_map = draw_leaf_map(jax.random.fold_in(streams_of[7], 71), 0)
    mid_map = draw_mid_map(jax.random.fold_in(streams_of[7], 71), 0)
    prior = jnp.clip(jnp.exp(math.log(4.0) - 1.3862944 * jax.random.uniform(streams_of[6], (LEAVES, 3, W), jnp.float32) ** steps_of(streams_of[6], (LEAVES, 3, W), ((0, 8),), -0.2, 0.2)), 1.0, 4.0)
    return dict(blocks=blocks, pattern=pattern, assign=assign, order=order, leaf_map=leaf_map, mid_map=mid_map, prior=prior)


def embed_rows(triangle, mapping):
    columns = (mapping[:, None] * BLK + jnp.arange(BLK, dtype=jnp.int32)[None, :]).reshape(-1)
    return jnp.zeros((triangle.shape[0], CB * BLK), jnp.float32).at[:, columns].set(triangle)

def stack_gram(upper_rows, lower_rows):
    stacked = jnp.concatenate([upper_rows, lower_rows], 0)
    return lax.dot_general(stacked.astype(jnp.float32), stacked.astype(jnp.float32), (((0,), (0,)), ((), ())), precision=lax.Precision.HIGHEST, preferred_element_type=jnp.float32)

def factor_front(gram, weights):
    lower = jnp.linalg.cholesky(gram + jnp.diag(weights))
    return lower.T

def reference(blocks, pattern, assign, order, leaf_map, mid_map, prior):
    full_width = CB * BLK
    half_width = full_width // 2
    quarter = full_width // 4
    colmask = jnp.repeat(pattern.astype(blocks.dtype), BLK, axis=1)
    masked = blocks * colmask[:, None, :]

    def add_block(grams, item):
        row_block, target = item
        widened = row_block.astype(jnp.float32)
        product = lax.dot_general(widened.astype(jnp.float32), widened.astype(jnp.float32), (((0,), (0,)), ((), ())), precision=lax.Precision.HIGHEST, preferred_element_type=jnp.float32)
        return (grams.at[target].add(product), None)
    grams, _ = lax.scan(add_block, jnp.zeros((LEAVES, full_width, full_width), jnp.float32), (masked, assign[:, 0]))
    leaf_rows = []
    contribs = []
    for slot in range(LEAVES):
        upper = factor_front(grams[order[slot]], prior[slot, 0])
        leaf_rows.append(upper[:half_width])
        contribs.append(upper[half_width:, half_width:])
    mid_rows = []
    mid_contribs = []
    for middle in range(LEAVES // 2):
        gram = stack_gram(embed_rows(contribs[2 * middle], leaf_map[2 * middle]), embed_rows(contribs[2 * middle + 1], leaf_map[2 * middle + 1]))
        upper = factor_front(gram, prior[2 * middle, 1] + prior[2 * middle + 1, 1])
        mid_rows.append(upper[:quarter])
        mid_rows.append(upper[quarter:half_width])
        mid_contribs.append(upper[half_width:, half_width:])
    top_rows = []
    for summit in range(LEAVES // 4):
        gram = stack_gram(embed_rows(mid_contribs[2 * summit], mid_map[2 * summit]), embed_rows(mid_contribs[2 * summit + 1], mid_map[2 * summit + 1]))
        weights = prior[4 * summit, 2] + prior[4 * summit + 1, 2] + (prior[4 * summit + 2, 2] + prior[4 * summit + 3, 2])
        upper = factor_front(gram, weights)
        for quad in range(4):
            top_rows.append(upper[quad * quarter:(quad + 1) * quarter])
    return (jnp.stack(leaf_rows), jnp.stack(mid_rows), jnp.stack(top_rows))
```

```python
import functools
import jax
import jax.numpy as jnp
from jax import lax
from jax.experimental import pallas as pl
from jax.experimental.pallas import tpu as pltpu
from jax.sharding import PartitionSpec as P

CAP = 2
SUB = 8
NEAR = 3
HIGHEST = lax.Precision.HIGHEST


def partner(value, axis, stride):
    mask = 2**stride
    pairs = [(source, source ^ mask) for source in range(lax.axis_size(axis))]
    return lax.ppermute(value, axis, pairs)


def lanes(tile, column):
    return jnp.broadcast_to(tile[:, column : column + 1], tile.shape)


def subs(tile, row):
    return jnp.broadcast_to(tile[row : row + 1, :], tile.shape)


def factor_tile(diagonal):
    size = diagonal.shape[0]
    tiles = size // SUB
    shape = (SUB, size)
    sub_ids = lax.broadcasted_iota(jnp.int32, shape, 0)
    lane_ids = lax.broadcasted_iota(jnp.int32, shape, 1)
    picks = [sub_ids == p for p in range(SUB)]
    left = [diagonal[SUB * t : SUB * (t + 1), :] for t in range(tiles)]
    right = [(lane_ids == sub_ids + SUB * t).astype(jnp.float32) for t in range(tiles)]
    zero = left[0] * 0.0
    upper, inverse = [], []

    def columns_of(t, step):
        return [lanes(left[t], SUB * step + j) for j in range(SUB)]

    own = [column + zero for column in columns_of(0, 0)]
    for step in range(tiles):
        own_left, own_right = left[step], right[step]
        row_left, row_right = own_left, own_right
        near = range(step + 1, min(step + 1 + NEAR, tiles))
        ahead = {t: columns_of(t, step) for t in near}
        following = None
        if step + 1 < tiles:
            following = [column + zero for column in columns_of(step + 1, step + 1)]
        for p in range(SUB):
            scale = lax.rsqrt(subs(own[p], p))
            squared = scale * scale
            ratio = [None] * SUB
            for k in range(p + 1, SUB):
                row = subs(own[k], p)
                ratio[k] = row * squared
                if k == p + 1:
                    own[k] = own[k] - (own[p] * row) * squared
                else:
                    own[k] = own[k] - own[p] * ratio[k]
            pivot_left, pivot_right = subs(own_left, p), subs(own_right, p)
            row_left = jnp.where(picks[p], pivot_left * scale, row_left)
            row_right = jnp.where(picks[p], pivot_right * scale, row_right)
            pivot_left, pivot_right = pivot_left * squared, pivot_right * squared
            if p < SUB - 1:
                own_left = own_left - own[p] * pivot_left
                own_right = own_right - own[p] * pivot_right
            if following is not None:
                scaled = ahead[step + 1][p] * squared
                for k in range(SUB):
                    following[k] = following[k] - ahead[step + 1][p] * subs(scaled, k)
            for t in near:
                left[t] = left[t] - ahead[t][p] * pivot_left
                right[t] = right[t] - ahead[t][p] * pivot_right
                for k in range(p + 1, SUB):
                    ahead[t][k] = ahead[t][k] - ahead[t][p] * ratio[k]
        upper.append(row_left)
        inverse.append(row_right)
        own = following
        if step + 1 + NEAR < tiles:
            high, low = halves(jnp.concatenate([row_left, row_right], 1))
            change = product((high[:, :size], low[:, :size]), (high, low), 0)
            for t in range(step + 1 + NEAR, tiles):
                rows = slice(SUB * t, SUB * (t + 1))
                left[t] = left[t] - change[rows, :size]
                right[t] = right[t] - change[rows, size:]
    return jnp.concatenate(upper, 0), jnp.concatenate(inverse, 0)


def halves(value):
    high = value.astype(jnp.bfloat16)
    return high, (value - high.astype(jnp.float32)).astype(jnp.bfloat16)


def product(left, right, contract):
    return lax.dot_general(
        jnp.concatenate([left[0], left[0], left[1]], contract),
        jnp.concatenate([right[0], right[1], right[0]], 0),
        (((contract,), (0,)), ((), ())),
        preferred_element_type=jnp.float32,
    )


def eliminate(front, split, pivots, block, touched=None):
    blocks = front.shape[0] // block

    def step(index, carry):
        start = pl.multiple_of(index * block, block)
        rows = pl.ds(start, block)

        def dense():
            upper, inverse = factor_tile(front[rows, rows])
            front[rows, :] = product(halves(inverse), halves(front[rows, :]), 1)
            front[rows, rows] = upper
            split[0], split[1] = halves(front[rows, :])

            def update(first, other, carry):
                below = pl.ds(pl.multiple_of(other * block, block), block)

                def apply():
                    front[below, first:] = front[below, first:] - product(
                        (split[0, :, below], split[1, :, below]), (split[0, :, first:], split[1, :, first:]), 0
                    )

                if touched is None:
                    apply()
                else:
                    pl.when(touched(other))(apply)
                return carry

            middle = blocks // 2
            lax.fori_loop(index + 1, middle, functools.partial(update, 0), 0)
            lax.fori_loop(
                jnp.maximum(index + 1, middle), blocks,
                functools.partial(update, middle * block), 0,
            )

        if touched is None:
            dense()
        else:
            here = touched(index)
            pl.when(here)(dense)

            @pl.when(jnp.logical_not(here))
            def _():
                tile = front[rows, rows]
                shape = (block, block)
                same = lax.broadcasted_iota(jnp.int32, shape, 0) == lax.broadcasted_iota(jnp.int32, shape, 1)
                front[rows, rows] = jnp.where(same, tile * lax.rsqrt(tile), 0.0)

        return carry

    lax.fori_loop(0, pivots // block, step, 0)


def add_weights(front, weights, block):
    size = front.shape[0]
    same = lax.broadcasted_iota(jnp.int32, (block, block), 0) == lax.broadcasted_iota(
        jnp.int32, (block, block), 1
    )
    for start in range(0, size, block):
        at = slice(start, start + block)
        front[at, at] = front[at, at] + jnp.where(same, weights[:, at], 0.0)


def take_rows(front, out, start):
    count, width = out.shape
    row_ids = start + lax.broadcasted_iota(jnp.int32, (count, width), 0)
    lane_ids = lax.broadcasted_iota(jnp.int32, (count, width), 1)
    out[...] = jnp.where(lane_ids >= row_ids, front[pl.ds(start, count), :], 0.0)


def pairs(count):
    return [(i, j) for i in range(count) for j in range(i, count)]


def pack_triangle(front, packed, first, block):
    count = front.shape[0] // block - first
    for index, (i, j) in enumerate(pairs(count)):
        rows, cols = (first + i) * block, (first + j) * block
        packed[index * block : (index + 1) * block, :] = front[
            rows : rows + block, cols : cols + block
        ]


def leaf_kernel(block, place, gram, weights, out, rest, front, split):
    width = front.shape[0]
    front[...] = jnp.zeros_like(front)
    for index, (i, j) in enumerate(pairs(width // block)):
        front[i * block : (i + 1) * block, j * block : (j + 1) * block] = gram[
            index * block : (index + 1) * block, :
        ]
    add_weights(front, weights, block)
    eliminate(front, split, width // 2, block)
    take_rows(front, out, pl.multiple_of(place[0] * out.shape[0], SUB))
    pack_triangle(front, rest, width // 2 // block, block)


def merge_kernel(block, pivots, place, maps, own, other, weights, out, *more):
    *more, front, split = more
    half = front.shape[0] // 2
    front[...] = jnp.zeros_like(front)
    add_weights(front, weights, block)
    for source, child in enumerate((own, other)):
        for index, (i, j) in enumerate(pairs(half // block)):
            tile = child[index * block : (index + 1) * block, :]
            first = pl.ds(pl.multiple_of(maps[source, i] * block, block), block)
            second = pl.ds(pl.multiple_of(maps[source, j] * block, block), block)
            front[first, second] = front[first, second] + tile
            if i != j:
                front[second, first] = front[second, first] + tile.T

    def touched(index):
        found = maps[0, 0] == index
        for source in range(2):
            for i in range(half // block):
                found = jnp.logical_or(found, maps[source, i] == index)
        return found

    eliminate(front, split, pivots, block, touched)
    take_rows(front, out, pl.multiple_of(place[0] * out.shape[0], SUB))
    if more:
        pack_triangle(front, more[0], half // block, block)


def gram_kernel(block, rows, packed):
    width = rows.shape[1]
    count = width // block
    where = {pair: index for index, pair in enumerate(pairs(count))}
    for i in range(0, count, 2):
        product = lax.dot_general(
            rows[:, i * block : (i + 2) * block], rows[:, i * block :],
            (((0,), (0,)), ((), ())), preferred_element_type=jnp.float32,
        )
        for k in (i, i + 1):
            for j in range(k, count):
                at = where[(k, j)] * block
                packed[at : at + block, :] = product[
                    (k - i) * block : (k - i + 1) * block, (j - i) * block : (j - i + 1) * block
                ]


def greet(devices):
    barrier = pltpu.get_barrier_semaphore()
    for device in devices:
        pl.semaphore_signal(
            barrier, inc=1, device_id=device, device_id_type=pl.DeviceIdType.MESH
        )
    pl.semaphore_wait(barrier, len(devices))


def remote(source, target, send, recv, device):
    copy = pltpu.make_async_remote_copy(
        src_ref=source, dst_ref=target, send_sem=send, recv_sem=recv,
        device_id=device, device_id_type=pl.DeviceIdType.MESH,
    )
    copy.start()
    return copy


def sum_kernel(fronts, part, out, total, full, landed, send, recv, send_back, recv_back):
    leaf, me = lax.axis_index("leaf"), lax.axis_index("front")
    strides = [2**level for level in range(fronts.bit_length() - 1)]
    sides = [lax.rem(me // stride, 2) for stride in strides]
    peers = [me + stride - 2 * stride * side for stride, side in zip(strides, sides)]
    levels = len(strides)
    half = part.shape[0] // 2
    orders = [list(range(levels)), list(reversed(range(levels)))]
    offset = [0, half]
    greet([(leaf, peer) for peer in peers])

    def at(start, size):
        return pl.ds(pl.multiple_of(start, SUB), size)

    size = half
    for level in range(levels):
        size = size // 2
        source = part if level == 0 else total
        copies, keeps = [], []
        for way in range(2):
            axis = orders[way][level]
            keeps.append(offset[way] + sides[axis] * size)
            slot = way * levels + level
            land = landed.at[pl.ds(way * half + half - 2 * size, size)]
            copies.append((
                remote(
                    source.at[at(offset[way] + (1 - sides[axis]) * size, size)], land,
                    send.at[slot], recv.at[slot], (leaf, peers[axis]),
                ),
                way * half + half - 2 * size,
            ))
        for way, (copy, place) in enumerate(copies):
            copy.wait()
            mine = at(keeps[way], size)
            result = full if level == levels - 1 else total
            result[mine, :] = source[mine, :] + landed[place : place + size, :]
            offset[way] = keeps[way]
    for level in reversed(range(levels)):
        copies = []
        for way in range(2):
            axis = orders[way][level]
            slot = way * levels + level
            mine = full.at[at(offset[way], size)]
            copies.append(
                remote(mine, mine, send_back.at[slot], recv_back.at[slot], (leaf, peers[axis]))
            )
            offset[way] = offset[way] - sides[axis] * size
        for copy in copies:
            copy.wait()
        size = size * 2
    out[...] = full[...]


def route_kernel(order, assign, pattern, blocks, out):
    leaves, positions = out.shape[:2]
    count, _, width = blocks.shape
    column_blocks = pattern.shape[1]
    block = width // column_blocks

    def slot_step(slot, carry):
        found = [jnp.int32(count)] * positions
        for b in range(count):
            free = assign[b] == order[slot]
            for p in range(positions):
                take = jnp.logical_and(free, found[p] == count)
                found[p] = jnp.where(take, b, found[p])
                free = jnp.logical_and(free, jnp.logical_not(take))
        for p in range(positions):
            source = jnp.minimum(found[p], count - 1)
            for c in range(column_blocks):
                keep = jnp.where(found[p] < count, pattern[source, c], 0)
                cols = slice(c * block, (c + 1) * block)
                scale = jnp.full((block, block), keep, jnp.int32).astype(jnp.float32)
                out[slot, p, :, cols] = blocks[source, :, cols] * scale.astype(out.dtype)
        return carry

    lax.fori_loop(0, leaves, slot_step, 0)


def swap_kernel(fronts, stride, own, out, got, send, recv, send_on, recv_on):
    leaf, me = lax.axis_index("leaf"), lax.axis_index("front")
    other = leaf + stride - 2 * stride * lax.rem(leaf // stride, 2)
    peers = [lax.rem(me + d, fronts) for d in range(1, fronts)]
    piece = own.shape[0] // fronts
    mine = pl.ds(pl.multiple_of(me * piece, SUB), piece)
    greet([(other, me)] + [(leaf, peer) for peer in peers])
    remote(own.at[mine], got.at[mine], send, recv, (other, me)).wait()
    copies = [
        remote(got.at[mine], got.at[mine], send_on.at[d], recv_on.at[d], (leaf, peer))
        for d, peer in enumerate(peers)
    ]
    for copy in copies:
        copy.wait()
    out[...] = got[...]


SMEM = pl.BlockSpec(memory_space=pltpu.SMEM)
VMEM = pl.BlockSpec(memory_space=pltpu.VMEM)


def route(order, assign, pattern, blocks, leaves):
    return pl.pallas_call(
        route_kernel,
        out_shape=jax.ShapeDtypeStruct((leaves, CAP) + blocks.shape[1:], blocks.dtype),
        in_specs=[SMEM, SMEM, SMEM, VMEM],
        out_specs=VMEM,
        compiler_params=pltpu.CompilerParams(vmem_limit_bytes=48 * 2**20),
        name="route_blocks",
    )(order, assign.reshape(-1), pattern, blocks)


def packed_gram(rows, block):
    count = rows.shape[1] // block
    return pl.pallas_call(
        functools.partial(gram_kernel, block),
        out_shape=jax.ShapeDtypeStruct((len(pairs(count)) * block, block), jnp.float32),
        in_specs=[VMEM],
        out_specs=VMEM,
        compiler_params=pltpu.CompilerParams(vmem_limit_bytes=48 * 2**20),
        name="packed_gram",
    )(rows)


def sum_fronts(part, fronts):
    size, width = part.shape
    many = pltpu.SemaphoreType.DMA((2 * (fronts.bit_length() - 1),))
    return pl.pallas_call(
        functools.partial(sum_kernel, fronts),
        out_shape=jax.ShapeDtypeStruct(part.shape, part.dtype),
        in_specs=[VMEM],
        out_specs=VMEM,
        scratch_shapes=[
            pltpu.VMEM((size, width), part.dtype),
            pltpu.VMEM((size, width), part.dtype),
            pltpu.VMEM((size, width), part.dtype),
            many, many, many, many,
        ],
        compiler_params=pltpu.CompilerParams(
            collective_id=0, has_side_effects=True, vmem_limit_bytes=48 * 2**20
        ),
        name="sum_fronts",
    )(part)


def swap_leaves(own, fronts, stride):
    many = pltpu.SemaphoreType.DMA((fronts - 1,))
    one = pltpu.SemaphoreType.DMA
    return pl.pallas_call(
        functools.partial(swap_kernel, fronts, stride),
        out_shape=jax.ShapeDtypeStruct(own.shape, own.dtype),
        in_specs=[VMEM],
        out_specs=VMEM,
        scratch_shapes=[pltpu.VMEM(own.shape, own.dtype), one, one, many, many],
        compiler_params=pltpu.CompilerParams(
            collective_id=1, has_side_effects=True, vmem_limit_bytes=48 * 2**20
        ),
        name="swap_leaves",
    )(own)


def triangle_shape(width, block):
    return jax.ShapeDtypeStruct((len(pairs(width // 2 // block)) * block, block), jnp.float32)


def leaf_level(gram, weights, place, rows, block):
    width = weights.shape[1]
    return pl.pallas_call(
        functools.partial(leaf_kernel, block),
        out_shape=(
            jax.ShapeDtypeStruct((rows, width), jnp.float32),
            triangle_shape(width, block),
        ),
        in_specs=[SMEM, VMEM, VMEM],
        out_specs=(VMEM, VMEM),
        scratch_shapes=[
            pltpu.VMEM((width, width), jnp.float32),
            pltpu.VMEM((2, block, width), jnp.bfloat16),
        ],
        compiler_params=pltpu.CompilerParams(vmem_limit_bytes=48 * 2**20),
        name="leaf_front",
    )(place.reshape(1).astype(jnp.int32), gram, weights)


def merge_level(own, other, maps, weights, place, rows, block, pivots, name):
    width = weights.shape[1]
    outs = [jax.ShapeDtypeStruct((rows, width), jnp.float32)]
    if pivots < width:
        outs.append(triangle_shape(width, block))
    return pl.pallas_call(
        functools.partial(merge_kernel, block, pivots),
        out_shape=tuple(outs),
        in_specs=[SMEM, SMEM, VMEM, VMEM, VMEM],
        out_specs=tuple([VMEM] * len(outs)),
        scratch_shapes=[
            pltpu.VMEM((width, width), jnp.float32),
            pltpu.VMEM((2, block, width), jnp.bfloat16),
        ],
        compiler_params=pltpu.CompilerParams(vmem_limit_bytes=48 * 2**20),
        name=name,
    )(place.reshape(1).astype(jnp.int32), maps, own, other, weights)


def local(blocks, pattern, assign, order, leaf_map, mid_map, prior):
    leaves = lax.axis_size("leaf")
    fronts = lax.axis_size("front")
    slot_index = lax.axis_index("leaf")
    front_index = lax.axis_index("front")
    local_blocks, block_size, full_width = blocks.shape
    half_width = full_width // 2
    quarter = full_width // 4
    carried = prior[0, 1:3]
    carried = carried + partner(carried, "leaf", 0)
    top_weights = carried[1:2] + partner(carried[1:2], "leaf", 1)
    outgoing = route(order, assign, pattern, blocks, leaves)
    arrived = lax.all_to_all(outgoing, "leaf", split_axis=0, concat_axis=0, tiled=True)
    arrived_rows = arrived.reshape(-1, full_width)
    gram = sum_fronts(packed_gram(arrived_rows, block_size), fronts)
    leaf_out, rest = leaf_level(
        gram, prior[0, 0:1], front_index, half_width // fronts, block_size
    )
    piece_rows = quarter // fronts
    partner_slot = jnp.bitwise_xor(slot_index, 1)
    mid_out, mid_rest = merge_level(
        rest,
        partner(rest, "leaf", 0),
        jnp.stack([leaf_map[slot_index], leaf_map[partner_slot]]),
        carried[0:1],
        slot_index % 2 * fronts + front_index,
        piece_rows,
        block_size,
        half_width,
        "mid_front",
    )
    middle = slot_index // 2
    other_middle = jnp.bitwise_xor(slot_index, 2) // 2
    (top_out,) = merge_level(
        mid_rest,
        swap_leaves(mid_rest, fronts, 2),
        jnp.stack([mid_map[middle], mid_map[other_middle]]),
        top_weights,
        slot_index % 4 * fronts + front_index,
        piece_rows,
        block_size,
        full_width,
        "top_front",
    )
    return (leaf_out[None], mid_out[None], top_out[None])


def solution(mesh):
    placed = (
        P(("leaf", "front"), None, None),
        P(("leaf", "front"), None),
        P(("leaf", "front"), None),
        P(),
        P(),
        P(),
        P("leaf", None, None),
    )
    return jax.shard_map(
        local,
        mesh=mesh,
        in_specs=placed,
        out_specs=(P("leaf", "front", None), P("leaf", "front", None), P("leaf", "front", None)),
        check_vma=False,
    )
```

```python
import functools
import jax
import jax.numpy as jnp
from jax import lax
from jax.experimental import pallas as pl
from jax.experimental.pallas import tpu as pltpu
from jax.sharding import PartitionSpec as P

CAP = 2
SUB = 8
NEAR = 3
HIGHEST = lax.Precision.HIGHEST


def partner(value, axis, stride):
    mask = 2**stride
    pairs = [(source, source ^ mask) for source in range(lax.axis_size(axis))]
    return lax.ppermute(value, axis, pairs)


def lanes(tile, column):
    return jnp.broadcast_to(tile[:, column : column + 1], tile.shape)


def subs(tile, row):
    return jnp.broadcast_to(tile[row : row + 1, :], tile.shape)


def factor_tile(diagonal):
    size = diagonal.shape[0]
    tiles = size // SUB
    shape = (SUB, size)
    sub_ids = lax.broadcasted_iota(jnp.int32, shape, 0)
    lane_ids = lax.broadcasted_iota(jnp.int32, shape, 1)
    picks = [sub_ids == p for p in range(SUB)]
    left = [diagonal[SUB * t : SUB * (t + 1), :] for t in range(tiles)]
    right = [(lane_ids == sub_ids + SUB * t).astype(jnp.float32) for t in range(tiles)]
    zero = left[0] * 0.0
    upper, inverse = [], []

    def columns_of(t, step):
        return [lanes(left[t], SUB * step + j) for j in range(SUB)]

    own = [column + zero for column in columns_of(0, 0)]
    for step in range(tiles):
        own_left, own_right = left[step], right[step]
        row_left, row_right = own_left, own_right
        near = range(step + 1, min(step + 1 + NEAR, tiles))
        ahead = {t: columns_of(t, step) for t in near}
        following = None
        if step + 1 < tiles:
            following = [column + zero for column in columns_of(step + 1, step + 1)]
        for p in range(SUB):
            scale = lax.rsqrt(subs(own[p], p))
            squared = scale * scale
            ratio = [None] * SUB
            for k in range(p + 1, SUB):
                row = subs(own[k], p)
                ratio[k] = row * squared
                if k == p + 1:
                    own[k] = own[k] - (own[p] * row) * squared
                else:
                    own[k] = own[k] - own[p] * ratio[k]
            pivot_left, pivot_right = subs(own_left, p), subs(own_right, p)
            row_left = jnp.where(picks[p], pivot_left * scale, row_left)
            row_right = jnp.where(picks[p], pivot_right * scale, row_right)
            pivot_left, pivot_right = pivot_left * squared, pivot_right * squared
            if p < SUB - 1:
                own_left = own_left - own[p] * pivot_left
                own_right = own_right - own[p] * pivot_right
            if following is not None:
                scaled = ahead[step + 1][p] * squared
                for k in range(SUB):
                    following[k] = following[k] - ahead[step + 1][p] * subs(scaled, k)
            for t in near:
                left[t] = left[t] - ahead[t][p] * pivot_left
                right[t] = right[t] - ahead[t][p] * pivot_right
                for k in range(p + 1, SUB):
                    ahead[t][k] = ahead[t][k] - ahead[t][p] * ratio[k]
        upper.append(row_left)
        inverse.append(row_right)
        own = following
        if step + 1 + NEAR < tiles:
            high, low = halves(jnp.concatenate([row_left, row_right], 1))
            change = product((high[:, :size], low[:, :size]), (high, low), 0)
            for t in range(step + 1 + NEAR, tiles):
                rows = slice(SUB * t, SUB * (t + 1))
                left[t] = left[t] - change[rows, :size]
                right[t] = right[t] - change[rows, size:]
    return jnp.concatenate(upper, 0), jnp.concatenate(inverse, 0)


def halves(value):
    high = value.astype(jnp.bfloat16)
    return high, (value - high.astype(jnp.float32)).astype(jnp.bfloat16)


def product(left, right, contract):
    return lax.dot_general(
        jnp.concatenate([left[0], left[0], left[1]], contract),
        jnp.concatenate([right[0], right[1], right[0]], 0),
        (((contract,), (0,)), ((), ())),
        preferred_element_type=jnp.float32,
    )


def eliminate(front, split, pivots, block, touched=None):
    blocks = front.shape[0] // block

    def step(index, carry):
        start = pl.multiple_of(index * block, block)
        rows = pl.ds(start, block)

        def dense():
            upper, inverse = factor_tile(front[rows, rows])
            front[rows, :] = product(halves(inverse), halves(front[rows, :]), 1)
            front[rows, rows] = upper
            split[0], split[1] = halves(front[rows, :])

            def update(first, other, carry):
                below = pl.ds(pl.multiple_of(other * block, block), block)

                def apply():
                    front[below, first:] = front[below, first:] - product(
                        (split[0, :, below], split[1, :, below]), (split[0, :, first:], split[1, :, first:]), 0
                    )

                if touched is None:
                    apply()
                else:
                    pl.when(touched(other))(apply)
                return carry

            middle = blocks // 2
            lax.fori_loop(index + 1, middle, functools.partial(update, 0), 0)
            lax.fori_loop(
                jnp.maximum(index + 1, middle), blocks,
                functools.partial(update, middle * block), 0,
            )

        if touched is None:
            dense()
        else:
            here = touched(index)
            pl.when(here)(dense)

            @pl.when(jnp.logical_not(here))
            def _():
                tile = front[rows, rows]
                shape = (block, block)
                same = lax.broadcasted_iota(jnp.int32, shape, 0) == lax.broadcasted_iota(jnp.int32, shape, 1)
                front[rows, rows] = jnp.where(same, tile * lax.rsqrt(tile), 0.0)

        return carry

    lax.fori_loop(0, pivots // block, step, 0)


def add_weights(front, weights, block):
    size = front.shape[0]
    same = lax.broadcasted_iota(jnp.int32, (block, block), 0) == lax.broadcasted_iota(
        jnp.int32, (block, block), 1
    )
    for start in range(0, size, block):
        at = slice(start, start + block)
        front[at, at] = front[at, at] + jnp.where(same, weights[:, at], 0.0)


def take_rows(front, out, start):
    count, width = out.shape
    row_ids = start + lax.broadcasted_iota(jnp.int32, (count, width), 0)
    lane_ids = lax.broadcasted_iota(jnp.int32, (count, width), 1)
    out[...] = jnp.where(lane_ids >= row_ids, front[pl.ds(start, count), :], 0.0)


def pairs(count):
    return [(i, j) for i in range(count) for j in range(i, count)]


def pack_triangle(front, packed, first, block):
    count = front.shape[0] // block - first
    for index, (i, j) in enumerate(pairs(count)):
        rows, cols = (first + i) * block, (first + j) * block
        packed[index * block : (index + 1) * block, :] = front[
            rows : rows + block, cols : cols + block
        ]


def leaf_kernel(block, place, gram, weights, out, rest, front, split):
    width = front.shape[0]
    front[...] = jnp.zeros_like(front)
    for index, (i, j) in enumerate(pairs(width // block)):
        front[i * block : (i + 1) * block, j * block : (j + 1) * block] = gram[
            index * block : (index + 1) * block, :
        ]
    add_weights(front, weights, block)
    eliminate(front, split, width // 2, block)
    take_rows(front, out, pl.multiple_of(place[0] * out.shape[0], SUB))
    pack_triangle(front, rest, width // 2 // block, block)


def merge_kernel(block, pivots, place, maps, own, other, weights, out, *more):
    *more, front, split = more
    half = front.shape[0] // 2
    front[...] = jnp.zeros_like(front)
    add_weights(front, weights, block)
    for source, child in enumerate((own, other)):
        for index, (i, j) in enumerate(pairs(half // block)):
            tile = child[index * block : (index + 1) * block, :]
            first = pl.ds(pl.multiple_of(maps[source, i] * block, block), block)
            second = pl.ds(pl.multiple_of(maps[source, j] * block, block), block)
            front[first, second] = front[first, second] + tile
            if i != j:
                front[second, first] = front[second, first] + tile.T

    def touched(index):
        found = maps[0, 0] == index
        for source in range(2):
            for i in range(half // block):
                found = jnp.logical_or(found, maps[source, i] == index)
        return found

    eliminate(front, split, pivots, block, touched)
    take_rows(front, out, pl.multiple_of(place[0] * out.shape[0], SUB))
    if more:
        pack_triangle(front, more[0], half // block, block)


def gram_tiles(block, rows, packed):
    width = rows.shape[1]
    count = width // block
    where = {pair: index for index, pair in enumerate(pairs(count))}
    for i in range(0, count, 2):
        product = lax.dot_general(
            rows[:, i * block : (i + 2) * block], rows[:, i * block :],
            (((0,), (0,)), ((), ())), preferred_element_type=jnp.float32,
        )
        for k in (i, i + 1):
            for j in range(k, count):
                at = where[(k, j)] * block
                packed[at : at + block, :] = product[
                    (k - i) * block : (k - i + 1) * block, (j - i) * block : (j - i + 1) * block
                ]


def greet(devices):
    barrier = pltpu.get_barrier_semaphore()
    for device in devices:
        pl.semaphore_signal(
            barrier, inc=1, device_id=device, device_id_type=pl.DeviceIdType.MESH
        )
    pl.semaphore_wait(barrier, len(devices))


def remote(source, target, send, recv, device):
    copy = pltpu.make_async_remote_copy(
        src_ref=source, dst_ref=target, send_sem=send, recv_sem=recv,
        device_id=device, device_id_type=pl.DeviceIdType.MESH,
    )
    copy.start()
    return copy


def sum_kernel(
    leaves, fronts, block, rows, out, far_rows, own_rows, far, own, landed, swapped, full,
    far_send, far_recv, own_send, own_recv, kept, send, recv, swap_send, swap_recv, send_back, recv_back,
):
    leaf, me = lax.axis_index("leaf"), lax.axis_index("front")
    team = leaves // 2
    side, mate = leaf // team, lax.rem(leaf, team)
    here, there = side * team, (1 - side) * team
    depth = far_rows.shape[0] // team
    strides = [2**level for level in range(fronts.bit_length() - 1)]
    sides = [lax.rem(me // stride, 2) for stride in strides]
    peers = [me + stride - 2 * stride * turn for stride, turn in zip(strides, sides)]
    levels = len(strides)
    half = far.shape[0] // 2
    orders = [list(range(levels)), list(reversed(range(levels)))]
    mates = [lax.rem(mate + d, team) for d in range(1, team)]
    opposite = there + mate
    greet([(here + other, me) for other in mates] + [(opposite, me)] + [(leaf, peer) for peer in peers])

    def at(start, size):
        return pl.ds(pl.multiple_of(start, SUB), size)

    def gather(base, target, send, recv, slot):
        place = target.at[at(mate * depth, depth)]
        copies = [
            remote(rows.at[at((base + other) * depth, depth)], place, send.at[d], recv.at[d], (here + other, me))
            for d, other in enumerate(mates)
        ]
        stay = pltpu.make_async_copy(rows.at[at((base + mate) * depth, depth)], place, kept.at[slot])
        stay.start()
        return copies + [stay]

    def scatter(part, which):
        offset = [0, half]
        size = half
        for level in range(levels):
            size = size // 2
            copies = []
            for way in range(2):
                axis = orders[way][level]
                keep = offset[way] + sides[axis] * size
                slot = (which * 2 + way) * levels + level
                place = way * half + half - 2 * size
                copies.append((
                    remote(
                        part.at[at(offset[way] + (1 - sides[axis]) * size, size)],
                        landed.at[which, pl.ds(place, size)],
                        send.at[slot], recv.at[slot], (leaf, peers[axis]),
                    ),
                    place,
                ))
                offset[way] = keep
            for way, (copy, place) in enumerate(copies):
                copy.wait()
                mine = at(offset[way], size)
                part[mine, :] = part[mine, :] + landed[which, place : place + size, :]
        return offset, size

    far_copies = gather(there, far_rows, far_send, far_recv, 0)
    own_copies = gather(here, own_rows, own_send, own_recv, 1)
    for copy in far_copies:
        copy.wait()
    gram_tiles(block, far_rows, far)
    offset, size = scatter(far, 0)
    swaps = [
        remote(
            far.at[at(offset[way], size)], swapped.at[pl.ds(way * size, size)],
            swap_send.at[way], swap_recv.at[way], (opposite, me),
        )
        for way in range(2)
    ]
    for copy in own_copies:
        copy.wait()
    gram_tiles(block, own_rows, own)
    offset, size = scatter(own, 1)
    for way, copy in enumerate(swaps):
        copy.wait()
        mine = at(offset[way], size)
        full[mine, :] = own[mine, :] + swapped[way * size : (way + 1) * size, :]
    for level in reversed(range(levels)):
        copies = []
        for way in range(2):
            axis = orders[way][level]
            slot = way * levels + level
            mine = full.at[at(offset[way], size)]
            copies.append(
                remote(mine, mine, send_back.at[slot], recv_back.at[slot], (leaf, peers[axis]))
            )
            offset[way] = offset[way] - sides[axis] * size
        for copy in copies:
            copy.wait()
        size = size * 2
    out[...] = full[...]


def route_kernel(order, assign, pattern, blocks, out):
    leaves, positions = out.shape[:2]
    count, _, width = blocks.shape
    column_blocks = pattern.shape[1]
    block = width // column_blocks

    def slot_step(slot, carry):
        found = [jnp.int32(count)] * positions
        for b in range(count):
            free = assign[b] == order[slot]
            for p in range(positions):
                take = jnp.logical_and(free, found[p] == count)
                found[p] = jnp.where(take, b, found[p])
                free = jnp.logical_and(free, jnp.logical_not(take))
        for p in range(positions):
            source = jnp.minimum(found[p], count - 1)
            for c in range(column_blocks):
                keep = jnp.where(found[p] < count, pattern[source, c], 0)
                cols = slice(c * block, (c + 1) * block)
                scale = jnp.full((block, block), keep, jnp.int32).astype(jnp.float32)
                out[slot, p, :, cols] = blocks[source, :, cols] * scale.astype(out.dtype)
        return carry

    lax.fori_loop(0, leaves, slot_step, 0)


def swap_kernel(fronts, stride, own, out, got, send, recv, send_on, recv_on):
    leaf, me = lax.axis_index("leaf"), lax.axis_index("front")
    other = leaf + stride - 2 * stride * lax.rem(leaf // stride, 2)
    peers = [lax.rem(me + d, fronts) for d in range(1, fronts)]
    piece = own.shape[0] // fronts
    mine = pl.ds(pl.multiple_of(me * piece, SUB), piece)
    greet([(other, me)] + [(leaf, peer) for peer in peers])
    remote(own.at[mine], got.at[mine], send, recv, (other, me)).wait()
    copies = [
        remote(got.at[mine], got.at[mine], send_on.at[d], recv_on.at[d], (leaf, peer))
        for d, peer in enumerate(peers)
    ]
    for copy in copies:
        copy.wait()
    out[...] = got[...]


SMEM = pl.BlockSpec(memory_space=pltpu.SMEM)
VMEM = pl.BlockSpec(memory_space=pltpu.VMEM)


def route(order, assign, pattern, blocks, leaves):
    return pl.pallas_call(
        route_kernel,
        out_shape=jax.ShapeDtypeStruct((leaves, CAP) + blocks.shape[1:], blocks.dtype),
        in_specs=[SMEM, SMEM, SMEM, VMEM],
        out_specs=VMEM,
        compiler_params=pltpu.CompilerParams(vmem_limit_bytes=48 * 2**20),
        name="route_blocks",
    )(order, assign.reshape(-1), pattern, blocks)


def gathered_gram(rows, leaves, fronts, block):
    width = rows.shape[1]
    packed = (len(pairs(width // block)) * block, block)
    team = leaves // 2
    levels = fronts.bit_length() - 1
    half_rows = (rows.shape[0] // 2, width)

    def many(count):
        return pltpu.SemaphoreType.DMA((count,))

    return pl.pallas_call(
        functools.partial(sum_kernel, leaves, fronts, block),
        out_shape=jax.ShapeDtypeStruct(packed, jnp.float32),
        in_specs=[VMEM],
        out_specs=VMEM,
        scratch_shapes=[
            pltpu.VMEM(half_rows, rows.dtype),
            pltpu.VMEM(half_rows, rows.dtype),
            pltpu.VMEM(packed, jnp.float32),
            pltpu.VMEM(packed, jnp.float32),
            pltpu.VMEM((2,) + packed, jnp.float32),
            pltpu.VMEM((packed[0] // fronts, block), jnp.float32),
            pltpu.VMEM(packed, jnp.float32),
            many(team - 1), many(team - 1), many(team - 1), many(team - 1), many(2),
            many(4 * levels), many(4 * levels), many(2), many(2),
            many(2 * levels), many(2 * levels),
        ],
        compiler_params=pltpu.CompilerParams(
            collective_id=0, has_side_effects=True, vmem_limit_bytes=56 * 2**20
        ),
        name="gathered_gram",
    )(rows)


def swap_leaves(own, fronts, stride):
    many = pltpu.SemaphoreType.DMA((fronts - 1,))
    one = pltpu.SemaphoreType.DMA
    return pl.pallas_call(
        functools.partial(swap_kernel, fronts, stride),
        out_shape=jax.ShapeDtypeStruct(own.shape, own.dtype),
        in_specs=[VMEM],
        out_specs=VMEM,
        scratch_shapes=[pltpu.VMEM(own.shape, own.dtype), one, one, many, many],
        compiler_params=pltpu.CompilerParams(
            collective_id=1, has_side_effects=True, vmem_limit_bytes=48 * 2**20
        ),
        name="swap_leaves",
    )(own)


def triangle_shape(width, block):
    return jax.ShapeDtypeStruct((len(pairs(width // 2 // block)) * block, block), jnp.float32)


def leaf_level(gram, weights, place, rows, block):
    width = weights.shape[1]
    return pl.pallas_call(
        functools.partial(leaf_kernel, block),
        out_shape=(
            jax.ShapeDtypeStruct((rows, width), jnp.float32),
            triangle_shape(width, block),
        ),
        in_specs=[SMEM, VMEM, VMEM],
        out_specs=(VMEM, VMEM),
        scratch_shapes=[
            pltpu.VMEM((width, width), jnp.float32),
            pltpu.VMEM((2, block, width), jnp.bfloat16),
        ],
        compiler_params=pltpu.CompilerParams(vmem_limit_bytes=48 * 2**20),
        name="leaf_front",
    )(place.reshape(1).astype(jnp.int32), gram, weights)


def merge_level(own, other, maps, weights, place, rows, block, pivots, name):
    width = weights.shape[1]
    outs = [jax.ShapeDtypeStruct((rows, width), jnp.float32)]
    if pivots < width:
        outs.append(triangle_shape(width, block))
    return pl.pallas_call(
        functools.partial(merge_kernel, block, pivots),
        out_shape=tuple(outs),
        in_specs=[SMEM, SMEM, VMEM, VMEM, VMEM],
        out_specs=tuple([VMEM] * len(outs)),
        scratch_shapes=[
            pltpu.VMEM((width, width), jnp.float32),
            pltpu.VMEM((2, block, width), jnp.bfloat16),
        ],
        compiler_params=pltpu.CompilerParams(vmem_limit_bytes=48 * 2**20),
        name=name,
    )(place.reshape(1).astype(jnp.int32), maps, own, other, weights)


def local(blocks, pattern, assign, order, leaf_map, mid_map, prior):
    leaves = lax.axis_size("leaf")
    fronts = lax.axis_size("front")
    slot_index = lax.axis_index("leaf")
    front_index = lax.axis_index("front")
    local_blocks, block_size, full_width = blocks.shape
    half_width = full_width // 2
    quarter = full_width // 4
    carried = prior[0, 1:3]
    carried = carried + partner(carried, "leaf", 0)
    top_weights = carried[1:2] + partner(carried[1:2], "leaf", 1)
    outgoing = route(order, assign, pattern, blocks, leaves)
    gram = gathered_gram(outgoing.reshape(-1, full_width), leaves, fronts, block_size)
    leaf_out, rest = leaf_level(
        gram, prior[0, 0:1], front_index, half_width // fronts, block_size
    )
    piece_rows = quarter // fronts
    partner_slot = jnp.bitwise_xor(slot_index, 1)
    mid_out, mid_rest = merge_level(
        rest,
        partner(rest, "leaf", 0),
        jnp.stack([leaf_map[slot_index], leaf_map[partner_slot]]),
        carried[0:1],
        slot_index % 2 * fronts + front_index,
        piece_rows,
        block_size,
        half_width,
        "mid_front",
    )
    middle = slot_index // 2
    other_middle = jnp.bitwise_xor(slot_index, 2) // 2
    (top_out,) = merge_level(
        mid_rest,
        swap_leaves(mid_rest, fronts, 2),
        jnp.stack([mid_map[middle], mid_map[other_middle]]),
        top_weights,
        slot_index % 4 * fronts + front_index,
        piece_rows,
        block_size,
        full_width,
        "top_front",
    )
    return (leaf_out[None], mid_out[None], top_out[None])


def solution(mesh):
    placed = (
        P(("leaf", "front"), None, None),
        P(("leaf", "front"), None),
        P(("leaf", "front"), None),
        P(),
        P(),
        P(),
        P("leaf", None, None),
    )
    return jax.shard_map(
        local,
        mesh=mesh,
        in_specs=placed,
        out_specs=(P("leaf", "front", None), P("leaf", "front", None), P("leaf", "front", None)),
        check_vma=False,
    )
```

```python
import functools
import jax
import jax.numpy as jnp
from jax import lax
from jax.experimental import pallas as pl
from jax.experimental.pallas import tpu as pltpu
from jax.sharding import PartitionSpec as P

CAP = 2
SUB = 8
NEAR = 3
HIGHEST = lax.Precision.HIGHEST


def partner(value, axis, stride):
    mask = 2**stride
    pairs = [(source, source ^ mask) for source in range(lax.axis_size(axis))]
    return lax.ppermute(value, axis, pairs)


def lanes(tile, column):
    return jnp.broadcast_to(tile[:, column : column + 1], tile.shape)


def subs(tile, row):
    return jnp.broadcast_to(tile[row : row + 1, :], tile.shape)


def factor_tile(diagonal):
    size = diagonal.shape[0]
    tiles = size // SUB
    shape = (SUB, size)
    sub_ids = lax.broadcasted_iota(jnp.int32, shape, 0)
    lane_ids = lax.broadcasted_iota(jnp.int32, shape, 1)
    picks = [sub_ids == p for p in range(SUB)]
    left = [diagonal[SUB * t : SUB * (t + 1), :] for t in range(tiles)]
    right = [(lane_ids == sub_ids + SUB * t).astype(jnp.float32) for t in range(tiles)]
    zero = left[0] * 0.0
    upper, inverse = [], []

    def columns_of(t, step):
        return [lanes(left[t], SUB * step + j) for j in range(SUB)]

    own = [column + zero for column in columns_of(0, 0)]
    for step in range(tiles):
        own_left, own_right = left[step], right[step]
        row_left, row_right = own_left, own_right
        near = range(step + 1, min(step + 1 + NEAR, tiles))
        ahead = {t: columns_of(t, step) for t in near}
        following = None
        if step + 1 < tiles:
            following = [column + zero for column in columns_of(step + 1, step + 1)]
        for p in range(SUB):
            scale = lax.rsqrt(subs(own[p], p))
            squared = scale * scale
            ratio = [None] * SUB
            for k in range(p + 1, SUB):
                row = subs(own[k], p)
                ratio[k] = row * squared
                if k == p + 1:
                    own[k] = own[k] - (own[p] * row) * squared
                else:
                    own[k] = own[k] - own[p] * ratio[k]
            pivot_left, pivot_right = subs(own_left, p), subs(own_right, p)
            row_left = jnp.where(picks[p], pivot_left * scale, row_left)
            row_right = jnp.where(picks[p], pivot_right * scale, row_right)
            pivot_left, pivot_right = pivot_left * squared, pivot_right * squared
            if p < SUB - 1:
                own_left = own_left - own[p] * pivot_left
                own_right = own_right - own[p] * pivot_right
            if following is not None:
                scaled = ahead[step + 1][p] * squared
                for k in range(SUB):
                    following[k] = following[k] - ahead[step + 1][p] * subs(scaled, k)
            for t in near:
                left[t] = left[t] - ahead[t][p] * pivot_left
                right[t] = right[t] - ahead[t][p] * pivot_right
                for k in range(p + 1, SUB):
                    ahead[t][k] = ahead[t][k] - ahead[t][p] * ratio[k]
        upper.append(row_left)
        inverse.append(row_right)
        own = following
        if step + 1 + NEAR < tiles:
            high, low = halves(jnp.concatenate([row_left, row_right], 1))
            change = product((high[:, :size], low[:, :size]), (high, low), 0)
            for t in range(step + 1 + NEAR, tiles):
                rows = slice(SUB * t, SUB * (t + 1))
                left[t] = left[t] - change[rows, :size]
                right[t] = right[t] - change[rows, size:]
    return jnp.concatenate(upper, 0), jnp.concatenate(inverse, 0)


def halves(value):
    high = value.astype(jnp.bfloat16)
    return high, (value - high.astype(jnp.float32)).astype(jnp.bfloat16)


def stacked(left, right, contract):
    return (
        jnp.concatenate([left[0], left[0], left[1]], contract),
        jnp.concatenate([right[0], right[1], right[0]], 0),
    )


def dot(left, right, contract):
    return lax.dot_general(
        left, right, (((contract,), (0,)), ((), ())), preferred_element_type=jnp.float32
    )


def product(left, right, contract):
    return dot(*stacked(left, right, contract), contract)


def eliminate(front, diagonal, over, under, pivots, block, touched=None):
    width = front.shape[0]
    blocks = width // block
    shape = (block, block)
    same = lax.broadcasted_iota(jnp.int32, shape, 0) == lax.broadcasted_iota(jnp.int32, shape, 1)
    lane_ids = lax.broadcasted_iota(jnp.int32, (block, width), 1)

    def put_off(first):
        start = first
        while start < blocks:
            stop = min(start + 2, blocks)
            rows = slice(start * block, stop * block)
            front[rows, start * block :] = front[rows, start * block :] - dot(
                over[:, rows], under[:, start * block :], 0
            )
            start = stop

    def step(first, index, carry):
        start = pl.multiple_of(index * block, block)
        rows = pl.ds(start, block)
        after = pl.ds(pl.multiple_of(jnp.minimum(index + 1, blocks - 1) * block, block), block)

        def dense():
            upper, inverse = factor_tile(diagonal[...])
            put_off(first)
            row = product(halves(inverse), halves(front[rows, :]), 1)
            front[rows, :] = row
            front[rows, rows] = upper
            parts = halves(jnp.where(lane_ids >= start + block, row, 0.0))
            over[...], under[...] = stacked(parts, parts, 0)
            diagonal[...] = front[after, after] - dot(over[:, after], under[:, after], 0)

        if touched is None:
            dense()
        else:
            here = touched(index)
            pl.when(here)(dense)

            @pl.when(jnp.logical_not(here))
            def _():
                put_off(first)
                tile = front[rows, rows]
                front[rows, rows] = jnp.where(same, tile * lax.rsqrt(tile), 0.0)
                over[...] = jnp.zeros_like(over)
                under[...] = jnp.zeros_like(under)
                diagonal[...] = front[after, after]

        return carry

    over[...] = jnp.zeros_like(over)
    under[...] = jnp.zeros_like(under)
    diagonal[...] = front[:block, :block]
    panels = pivots // block
    middle = min(panels, blocks // 2)
    lax.fori_loop(0, middle, functools.partial(step, 1), 0)
    if middle < panels:
        lax.fori_loop(middle, panels, functools.partial(step, middle), 0)
    put_off(panels)


def work(width, block):
    return [
        pltpu.VMEM((width, width), jnp.float32),
        pltpu.VMEM((block, block), jnp.float32),
        pltpu.VMEM((3 * block, width), jnp.bfloat16),
        pltpu.VMEM((3 * block, width), jnp.bfloat16),
    ]


def add_weights(front, weights, block):
    size = front.shape[0]
    same = lax.broadcasted_iota(jnp.int32, (block, block), 0) == lax.broadcasted_iota(
        jnp.int32, (block, block), 1
    )
    for start in range(0, size, block):
        at = slice(start, start + block)
        front[at, at] = front[at, at] + jnp.where(same, weights[:, at], 0.0)


def take_rows(front, out, start):
    count, width = out.shape
    row_ids = start + lax.broadcasted_iota(jnp.int32, (count, width), 0)
    lane_ids = lax.broadcasted_iota(jnp.int32, (count, width), 1)
    out[...] = jnp.where(lane_ids >= row_ids, front[pl.ds(start, count), :], 0.0)


def pairs(count):
    return [(i, j) for i in range(count) for j in range(i, count)]


def pack_triangle(front, packed, first, block):
    count = front.shape[0] // block - first
    for index, (i, j) in enumerate(pairs(count)):
        rows, cols = (first + i) * block, (first + j) * block
        packed[index * block : (index + 1) * block, :] = front[
            rows : rows + block, cols : cols + block
        ]


def leaf_kernel(block, place, gram, weights, out, rest, front, diagonal, over, under):
    width = front.shape[0]
    front[...] = jnp.zeros_like(front)
    for index, (i, j) in enumerate(pairs(width // block)):
        front[i * block : (i + 1) * block, j * block : (j + 1) * block] = gram[
            index * block : (index + 1) * block, :
        ]
    add_weights(front, weights, block)
    eliminate(front, diagonal, over, under, width // 2, block)
    take_rows(front, out, pl.multiple_of(place[0] * out.shape[0], SUB))
    pack_triangle(front, rest, width // 2 // block, block)


def merge_kernel(block, pivots, place, maps, own, other, weights, out, *more):
    *more, front, diagonal, over, under = more
    half = front.shape[0] // 2
    front[...] = jnp.zeros_like(front)
    add_weights(front, weights, block)
    for source, child in enumerate((own, other)):
        for index, (i, j) in enumerate(pairs(half // block)):
            tile = child[index * block : (index + 1) * block, :]
            first = pl.ds(pl.multiple_of(maps[source, i] * block, block), block)
            second = pl.ds(pl.multiple_of(maps[source, j] * block, block), block)
            front[first, second] = front[first, second] + tile
            if i != j:
                front[second, first] = front[second, first] + tile.T

    def touched(index):
        found = maps[0, 0] == index
        for source in range(2):
            for i in range(half // block):
                found = jnp.logical_or(found, maps[source, i] == index)
        return found

    eliminate(front, diagonal, over, under, pivots, block, touched)
    take_rows(front, out, pl.multiple_of(place[0] * out.shape[0], SUB))
    if more:
        pack_triangle(front, more[0], half // block, block)


def gram_tiles(block, rows, packed):
    width = rows.shape[1]
    count = width // block
    where = {pair: index for index, pair in enumerate(pairs(count))}
    for i in range(0, count, 2):
        product = lax.dot_general(
            rows[:, i * block : (i + 2) * block], rows[:, i * block :],
            (((0,), (0,)), ((), ())), preferred_element_type=jnp.float32,
        )
        for k in (i, i + 1):
            for j in range(k, count):
                at = where[(k, j)] * block
                packed[at : at + block, :] = product[
                    (k - i) * block : (k - i + 1) * block, (j - i) * block : (j - i + 1) * block
                ]


def greet(devices):
    barrier = pltpu.get_barrier_semaphore()
    for device in devices:
        pl.semaphore_signal(
            barrier, inc=1, device_id=device, device_id_type=pl.DeviceIdType.MESH
        )
    pl.semaphore_wait(barrier, len(devices))


def remote(source, target, send, recv, device):
    copy = pltpu.make_async_remote_copy(
        src_ref=source, dst_ref=target, send_sem=send, recv_sem=recv,
        device_id=device, device_id_type=pl.DeviceIdType.MESH,
    )
    copy.start()
    return copy


def sum_kernel(
    leaves, fronts, block, rows, out, far_rows, own_rows, far, own, landed, swapped, full,
    far_send, far_recv, own_send, own_recv, kept, send, recv, swap_send, swap_recv, send_back, recv_back,
):
    leaf, me = lax.axis_index("leaf"), lax.axis_index("front")
    team = leaves // 2
    side, mate = leaf // team, lax.rem(leaf, team)
    here, there = side * team, (1 - side) * team
    depth = far_rows.shape[0] // team
    strides = [2**level for level in range(fronts.bit_length() - 1)]
    sides = [lax.rem(me // stride, 2) for stride in strides]
    peers = [me + stride - 2 * stride * turn for stride, turn in zip(strides, sides)]
    levels = len(strides)
    half = far.shape[0] // 2
    orders = [list(range(levels)), list(reversed(range(levels)))]
    mates = [lax.rem(mate + d, team) for d in range(1, team)]
    opposite = there + mate
    greet([(here + other, me) for other in mates] + [(opposite, me)] + [(leaf, peer) for peer in peers])

    def at(start, size):
        return pl.ds(pl.multiple_of(start, SUB), size)

    def gather(base, target, send, recv, slot):
        place = target.at[at(mate * depth, depth)]
        copies = [
            remote(rows.at[at((base + other) * depth, depth)], place, send.at[d], recv.at[d], (here + other, me))
            for d, other in enumerate(mates)
        ]
        stay = pltpu.make_async_copy(rows.at[at((base + mate) * depth, depth)], place, kept.at[slot])
        stay.start()
        return copies + [stay]

    def scatter(part, which):
        offset = [0, half]
        size = half
        for level in range(levels):
            size = size // 2
            copies = []
            for way in range(2):
                axis = orders[way][level]
                keep = offset[way] + sides[axis] * size
                slot = (which * 2 + way) * levels + level
                place = way * half + half - 2 * size
                copies.append((
                    remote(
                        part.at[at(offset[way] + (1 - sides[axis]) * size, size)],
                        landed.at[which, pl.ds(place, size)],
                        send.at[slot], recv.at[slot], (leaf, peers[axis]),
                    ),
                    place,
                ))
                offset[way] = keep
            for way, (copy, place) in enumerate(copies):
                copy.wait()
                mine = at(offset[way], size)
                part[mine, :] = part[mine, :] + landed[which, place : place + size, :]
        return offset, size

    far_copies = gather(there, far_rows, far_send, far_recv, 0)
    own_copies = gather(here, own_rows, own_send, own_recv, 1)
    for copy in far_copies:
        copy.wait()
    gram_tiles(block, far_rows, far)
    offset, size = scatter(far, 0)
    swaps = [
        remote(
            far.at[at(offset[way], size)], swapped.at[pl.ds(way * size, size)],
            swap_send.at[way], swap_recv.at[way], (opposite, me),
        )
        for way in range(2)
    ]
    for copy in own_copies:
        copy.wait()
    gram_tiles(block, own_rows, own)
    offset, size = scatter(own, 1)
    for way, copy in enumerate(swaps):
        copy.wait()
        mine = at(offset[way], size)
        full[mine, :] = own[mine, :] + swapped[way * size : (way + 1) * size, :]
    for level in reversed(range(levels)):
        copies = []
        for way in range(2):
            axis = orders[way][level]
            slot = way * levels + level
            mine = full.at[at(offset[way], size)]
            copies.append(
                remote(mine, mine, send_back.at[slot], recv_back.at[slot], (leaf, peers[axis]))
            )
            offset[way] = offset[way] - sides[axis] * size
        for copy in copies:
            copy.wait()
        size = size * 2
    out[...] = full[...]


def route_kernel(order, assign, pattern, blocks, out):
    leaves, positions = out.shape[:2]
    count, _, width = blocks.shape
    column_blocks = pattern.shape[1]
    block = width // column_blocks

    def slot_step(slot, carry):
        found = [jnp.int32(count)] * positions
        for b in range(count):
            free = assign[b] == order[slot]
            for p in range(positions):
                take = jnp.logical_and(free, found[p] == count)
                found[p] = jnp.where(take, b, found[p])
                free = jnp.logical_and(free, jnp.logical_not(take))
        for p in range(positions):
            source = jnp.minimum(found[p], count - 1)
            for c in range(column_blocks):
                keep = jnp.where(found[p] < count, pattern[source, c], 0)
                cols = slice(c * block, (c + 1) * block)
                scale = jnp.full((block, block), keep, jnp.int32).astype(jnp.float32)
                out[slot, p, :, cols] = blocks[source, :, cols] * scale.astype(out.dtype)
        return carry

    lax.fori_loop(0, leaves, slot_step, 0)


def swap_kernel(fronts, stride, own, out, got, send, recv, send_on, recv_on):
    leaf, me = lax.axis_index("leaf"), lax.axis_index("front")
    other = leaf + stride - 2 * stride * lax.rem(leaf // stride, 2)
    peers = [lax.rem(me + d, fronts) for d in range(1, fronts)]
    piece = own.shape[0] // fronts
    mine = pl.ds(pl.multiple_of(me * piece, SUB), piece)
    greet([(other, me)] + [(leaf, peer) for peer in peers])
    remote(own.at[mine], got.at[mine], send, recv, (other, me)).wait()
    copies = [
        remote(got.at[mine], got.at[mine], send_on.at[d], recv_on.at[d], (leaf, peer))
        for d, peer in enumerate(peers)
    ]
    for copy in copies:
        copy.wait()
    out[...] = got[...]


SMEM = pl.BlockSpec(memory_space=pltpu.SMEM)
VMEM = pl.BlockSpec(memory_space=pltpu.VMEM)


def route(order, assign, pattern, blocks, leaves):
    return pl.pallas_call(
        route_kernel,
        out_shape=jax.ShapeDtypeStruct((leaves, CAP) + blocks.shape[1:], blocks.dtype),
        in_specs=[SMEM, SMEM, SMEM, VMEM],
        out_specs=VMEM,
        compiler_params=pltpu.CompilerParams(vmem_limit_bytes=48 * 2**20),
        name="route_blocks",
    )(order, assign.reshape(-1), pattern, blocks)


def gathered_gram(rows, leaves, fronts, block):
    width = rows.shape[1]
    packed = (len(pairs(width // block)) * block, block)
    team = leaves // 2
    levels = fronts.bit_length() - 1
    half_rows = (rows.shape[0] // 2, width)

    def many(count):
        return pltpu.SemaphoreType.DMA((count,))

    return pl.pallas_call(
        functools.partial(sum_kernel, leaves, fronts, block),
        out_shape=jax.ShapeDtypeStruct(packed, jnp.float32),
        in_specs=[VMEM],
        out_specs=VMEM,
        scratch_shapes=[
            pltpu.VMEM(half_rows, rows.dtype),
            pltpu.VMEM(half_rows, rows.dtype),
            pltpu.VMEM(packed, jnp.float32),
            pltpu.VMEM(packed, jnp.float32),
            pltpu.VMEM((2,) + packed, jnp.float32),
            pltpu.VMEM((packed[0] // fronts, block), jnp.float32),
            pltpu.VMEM(packed, jnp.float32),
            many(team - 1), many(team - 1), many(team - 1), many(team - 1), many(2),
            many(4 * levels), many(4 * levels), many(2), many(2),
            many(2 * levels), many(2 * levels),
        ],
        compiler_params=pltpu.CompilerParams(
            collective_id=0, has_side_effects=True, vmem_limit_bytes=56 * 2**20
        ),
        name="gathered_gram",
    )(rows)


def swap_leaves(own, fronts, stride):
    many = pltpu.SemaphoreType.DMA((fronts - 1,))
    one = pltpu.SemaphoreType.DMA
    return pl.pallas_call(
        functools.partial(swap_kernel, fronts, stride),
        out_shape=jax.ShapeDtypeStruct(own.shape, own.dtype),
        in_specs=[VMEM],
        out_specs=VMEM,
        scratch_shapes=[pltpu.VMEM(own.shape, own.dtype), one, one, many, many],
        compiler_params=pltpu.CompilerParams(
            collective_id=1, has_side_effects=True, vmem_limit_bytes=48 * 2**20
        ),
        name="swap_leaves",
    )(own)


def triangle_shape(width, block):
    return jax.ShapeDtypeStruct((len(pairs(width // 2 // block)) * block, block), jnp.float32)


def leaf_level(gram, weights, place, rows, block):
    width = weights.shape[1]
    return pl.pallas_call(
        functools.partial(leaf_kernel, block),
        out_shape=(
            jax.ShapeDtypeStruct((rows, width), jnp.float32),
            triangle_shape(width, block),
        ),
        in_specs=[SMEM, VMEM, VMEM],
        out_specs=(VMEM, VMEM),
        scratch_shapes=work(width, block),
        compiler_params=pltpu.CompilerParams(vmem_limit_bytes=48 * 2**20),
        name="leaf_front",
    )(place.reshape(1).astype(jnp.int32), gram, weights)


def merge_level(own, other, maps, weights, place, rows, block, pivots, name):
    width = weights.shape[1]
    outs = [jax.ShapeDtypeStruct((rows, width), jnp.float32)]
    if pivots < width:
        outs.append(triangle_shape(width, block))
    return pl.pallas_call(
        functools.partial(merge_kernel, block, pivots),
        out_shape=tuple(outs),
        in_specs=[SMEM, SMEM, VMEM, VMEM, VMEM],
        out_specs=tuple([VMEM] * len(outs)),
        scratch_shapes=work(width, block),
        compiler_params=pltpu.CompilerParams(vmem_limit_bytes=48 * 2**20),
        name=name,
    )(place.reshape(1).astype(jnp.int32), maps, own, other, weights)


def local(blocks, pattern, assign, order, leaf_map, mid_map, prior):
    leaves = lax.axis_size("leaf")
    fronts = lax.axis_size("front")
    slot_index = lax.axis_index("leaf")
    front_index = lax.axis_index("front")
    local_blocks, block_size, full_width = blocks.shape
    half_width = full_width // 2
    quarter = full_width // 4
    carried = prior[0, 1:3]
    carried = carried + partner(carried, "leaf", 0)
    top_weights = carried[1:2] + partner(carried[1:2], "leaf", 1)
    outgoing = route(order, assign, pattern, blocks, leaves)
    gram = gathered_gram(outgoing.reshape(-1, full_width), leaves, fronts, block_size)
    leaf_out, rest = leaf_level(
        gram, prior[0, 0:1], front_index, half_width // fronts, block_size
    )
    piece_rows = quarter // fronts
    partner_slot = jnp.bitwise_xor(slot_index, 1)
    mid_out, mid_rest = merge_level(
        rest,
        partner(rest, "leaf", 0),
        jnp.stack([leaf_map[slot_index], leaf_map[partner_slot]]),
        carried[0:1],
        slot_index % 2 * fronts + front_index,
        piece_rows,
        block_size,
        half_width,
        "mid_front",
    )
    middle = slot_index // 2
    other_middle = jnp.bitwise_xor(slot_index, 2) // 2
    (top_out,) = merge_level(
        mid_rest,
        swap_leaves(mid_rest, fronts, 2),
        jnp.stack([mid_map[middle], mid_map[other_middle]]),
        top_weights,
        slot_index % 4 * fronts + front_index,
        piece_rows,
        block_size,
        full_width,
        "top_front",
    )
    return (leaf_out[None], mid_out[None], top_out[None])


def solution(mesh):
    placed = (
        P(("leaf", "front"), None, None),
        P(("leaf", "front"), None),
        P(("leaf", "front"), None),
        P(),
        P(),
        P(),
        P("leaf", None, None),
    )
    return jax.shard_map(
        local,
        mesh=mesh,
        in_specs=placed,
        out_specs=(P("leaf", "front", None), P("leaf", "front", None), P("leaf", "front", None)),
        check_vma=False,
    )
```

```python
import functools
import jax
import jax.numpy as jnp
from jax import lax
from jax.experimental import pallas as pl
from jax.experimental.pallas import tpu as pltpu
from jax.sharding import PartitionSpec as P

CAP = 2
SUB = 8
NEAR = 3
HIGHEST = lax.Precision.HIGHEST


def partner(value, axis, stride):
    mask = 2**stride
    pairs = [(source, source ^ mask) for source in range(lax.axis_size(axis))]
    return lax.ppermute(value, axis, pairs)


def lanes(tile, column):
    return jnp.broadcast_to(tile[:, column : column + 1], tile.shape)


def subs(tile, row):
    return jnp.broadcast_to(tile[row : row + 1, :], tile.shape)


def factor_tile(diagonal):
    size = diagonal.shape[0]
    tiles = size // SUB
    shape = (SUB, size)
    sub_ids = lax.broadcasted_iota(jnp.int32, shape, 0)
    lane_ids = lax.broadcasted_iota(jnp.int32, shape, 1)
    picks = [sub_ids == p for p in range(SUB)]
    left = [diagonal[SUB * t : SUB * (t + 1), :] for t in range(tiles)]
    right = [(lane_ids == sub_ids + SUB * t).astype(jnp.float32) for t in range(tiles)]
    zero = left[0] * 0.0
    upper, inverse = [], []

    def columns_of(t, step):
        return [lanes(left[t], SUB * step + j) for j in range(SUB)]

    own = [column + zero for column in columns_of(0, 0)]
    for step in range(tiles):
        own_left, own_right = left[step], right[step]
        row_left, row_right = own_left, own_right
        near = range(step + 1, min(step + 1 + NEAR, tiles))
        ahead = {t: columns_of(t, step) for t in near}
        following = None
        if step + 1 < tiles:
            following = [column + zero for column in columns_of(step + 1, step + 1)]
        for p in range(SUB):
            scale = lax.rsqrt(subs(own[p], p))
            squared = scale * scale
            ratio = [None] * SUB
            for k in range(p + 1, SUB):
                row = subs(own[k], p)
                ratio[k] = row * squared
                if k == p + 1:
                    own[k] = own[k] - (own[p] * row) * squared
                else:
                    own[k] = own[k] - own[p] * ratio[k]
            pivot_left, pivot_right = subs(own_left, p), subs(own_right, p)
            row_left = jnp.where(picks[p], pivot_left * scale, row_left)
            row_right = jnp.where(picks[p], pivot_right * scale, row_right)
            pivot_left, pivot_right = pivot_left * squared, pivot_right * squared
            if p < SUB - 1:
                own_left = own_left - own[p] * pivot_left
                own_right = own_right - own[p] * pivot_right
            if following is not None:
                scaled = ahead[step + 1][p] * squared
                for k in range(SUB):
                    following[k] = following[k] - ahead[step + 1][p] * subs(scaled, k)
            for t in near:
                left[t] = left[t] - ahead[t][p] * pivot_left
                right[t] = right[t] - ahead[t][p] * pivot_right
                for k in range(p + 1, SUB):
                    ahead[t][k] = ahead[t][k] - ahead[t][p] * ratio[k]
        upper.append(row_left)
        inverse.append(row_right)
        own = following
        if step + 1 + NEAR < tiles:
            high, low = halves(jnp.concatenate([row_left, row_right], 1))
            change = product((high[:, :size], low[:, :size]), (high, low), 0)
            for t in range(step + 1 + NEAR, tiles):
                rows = slice(SUB * t, SUB * (t + 1))
                left[t] = left[t] - change[rows, :size]
                right[t] = right[t] - change[rows, size:]
    return jnp.concatenate(upper, 0), jnp.concatenate(inverse, 0)


def halves(value):
    high = value.astype(jnp.bfloat16)
    return high, (value - high.astype(jnp.float32)).astype(jnp.bfloat16)


def stacked(left, right, contract):
    return (
        jnp.concatenate([left[0], left[0], left[1]], contract),
        jnp.concatenate([right[0], right[1], right[0]], 0),
    )


def dot(left, right, contract):
    return lax.dot_general(
        left, right, (((contract,), (0,)), ((), ())), preferred_element_type=jnp.float32
    )


def product(left, right, contract):
    return dot(*stacked(left, right, contract), contract)


def eliminate(front, diagonal, over, under, pivots, block, touched=None):
    width = front.shape[0]
    blocks = width // block
    shape = (block, block)
    same = lax.broadcasted_iota(jnp.int32, shape, 0) == lax.broadcasted_iota(jnp.int32, shape, 1)
    lane_ids = lax.broadcasted_iota(jnp.int32, (block, width), 1)

    def put_off(first):
        start = first
        while start < blocks:
            stop = min(start + 2, blocks)
            rows = slice(start * block, stop * block)
            front[rows, start * block :] = front[rows, start * block :] - dot(
                over[:, rows], under[:, start * block :], 0
            )
            start = stop

    def step(first, index, carry):
        start = pl.multiple_of(index * block, block)
        rows = pl.ds(start, block)
        after = pl.ds(pl.multiple_of(jnp.minimum(index + 1, blocks - 1) * block, block), block)

        def dense():
            upper, inverse = factor_tile(diagonal[...])
            put_off(first)
            row = product(halves(inverse), halves(front[rows, :]), 1)
            front[rows, :] = row
            front[rows, rows] = upper
            parts = halves(jnp.where(lane_ids >= start + block, row, 0.0))
            over[...], under[...] = stacked(parts, parts, 0)
            diagonal[...] = front[after, after] - dot(over[:, after], under[:, after], 0)

        if touched is None:
            dense()
        else:
            here = touched(index)
            pl.when(here)(dense)

            @pl.when(jnp.logical_not(here))
            def _():
                put_off(first)
                tile = front[rows, rows]
                front[rows, rows] = jnp.where(same, tile * lax.rsqrt(tile), 0.0)
                over[...] = jnp.zeros_like(over)
                under[...] = jnp.zeros_like(under)
                diagonal[...] = front[after, after]

        return carry

    over[...] = jnp.zeros_like(over)
    under[...] = jnp.zeros_like(under)
    diagonal[...] = front[:block, :block]
    panels = pivots // block
    middle = min(panels, blocks // 2)
    lax.fori_loop(0, middle, functools.partial(step, 1), 0)
    if middle < panels:
        lax.fori_loop(middle, panels, functools.partial(step, middle), 0)
    put_off(panels)


def work(width, block):
    return [
        pltpu.VMEM((width, width), jnp.float32),
        pltpu.VMEM((block, block), jnp.float32),
        pltpu.VMEM((3 * block, width), jnp.bfloat16),
        pltpu.VMEM((3 * block, width), jnp.bfloat16),
    ]


def add_weights(front, weight_of, block):
    size = front.shape[0]
    same = lax.broadcasted_iota(jnp.int32, (block, block), 0) == lax.broadcasted_iota(
        jnp.int32, (block, block), 1
    )
    for start in range(0, size, block):
        at = slice(start, start + block)
        front[at, at] = front[at, at] + jnp.where(same, weight_of(start // block), 0.0)


def take_rows(front, out, start):
    count, width = out.shape
    row_ids = start + lax.broadcasted_iota(jnp.int32, (count, width), 0)
    lane_ids = lax.broadcasted_iota(jnp.int32, (count, width), 1)
    out[...] = jnp.where(lane_ids >= row_ids, front[pl.ds(start, count), :], 0.0)


def pairs(count):
    return [(i, j) for i in range(count) for j in range(i, count)]


def pack_triangle(front, packed, first, block):
    count = front.shape[0] // block - first
    for index, (i, j) in enumerate(pairs(count)):
        rows, cols = (first + i) * block, (first + j) * block
        packed[index * block : (index + 1) * block, :] = front[
            rows : rows + block, cols : cols + block
        ]


def carry_rows(packed, base, rows):
    packed[base:, :] = jnp.zeros((packed.shape[0] - base, packed.shape[1]), packed.dtype)
    for index, row in enumerate(rows):
        packed[base + index : base + index + 1, :] = row


def leaf_kernel(block, gram, weights, out, rest, front, diagonal, over, under):
    width = front.shape[0]
    blocks = width // block
    for index, (i, j) in enumerate(pairs(blocks)):
        front[i * block : (i + 1) * block, j * block : (j + 1) * block] = gram[
            index * block : (index + 1) * block, :
        ]

    def weight_of(level, b):
        return weights[level : level + 1, b * block : (b + 1) * block]

    add_weights(front, functools.partial(weight_of, 0), block)
    base = len(pairs(blocks // 2)) * block
    carry_rows(rest, base, [weight_of(level, b) for level in (1, 2) for b in range(blocks)])
    eliminate(front, diagonal, over, under, width // 2, block)
    take_rows(front, out, pl.multiple_of(lax.axis_index("front") * out.shape[0], SUB))
    pack_triangle(front, rest, blocks // 2, block)


def merge_kernel(block, pivots, fronts, level, maps, own, other, out, *more):
    *more, front, diagonal, over, under = more
    width = front.shape[0]
    half = width // 2
    blocks = width // block
    base = len(pairs(blocks // 2)) * block
    leaf = lax.axis_index("leaf")
    below = 2 ** (level - 1)
    mine = leaf // below
    theirs = mine + 1 - 2 * lax.rem(mine, 2)
    front[...] = jnp.zeros_like(front)
    add_weights(front, lambda b: own[base + b : base + b + 1, :] + other[base + b : base + b + 1, :], block)
    for source, child in ((mine, own), (theirs, other)):
        for index, (i, j) in enumerate(pairs(half // block)):
            tile = child[index * block : (index + 1) * block, :]
            row, column = maps[source, i], maps[source, j]
            first = pl.ds(pl.multiple_of(row * block, block), block)
            second = pl.ds(pl.multiple_of(column * block, block), block)

            def plain(first=first, second=second, tile=tile):
                front[first, second] = front[first, second] + tile

            def turned(first=first, second=second, tile=tile):
                front[second, first] = front[second, first] + tile.T

            if i == j:
                plain()
            else:
                pl.when(row < column)(plain)
                pl.when(row > column)(turned)

    def touched(index):
        found = maps[mine, 0] == index
        for source in (mine, theirs):
            for i in range(half // block):
                found = jnp.logical_or(found, maps[source, i] == index)
        return found

    eliminate(front, diagonal, over, under, pivots, block, touched)
    turn = lax.rem(leaf, 2**level) * fronts + lax.axis_index("front")
    take_rows(front, out, pl.multiple_of(turn * out.shape[0], SUB))
    if more:
        carry_rows(more[0], base, [
            own[base + b : base + b + 1, :] + other[base + b : base + b + 1, :]
            for b in range(blocks, 2 * blocks)
        ])
        pack_triangle(front, more[0], half // block, block)


def gram_tiles(block, rows, packed):
    width = rows.shape[1]
    count = width // block
    where = {pair: index for index, pair in enumerate(pairs(count))}
    for i in range(0, count, 2):
        product = lax.dot_general(
            rows[:, i * block : (i + 2) * block], rows[:, i * block :],
            (((0,), (0,)), ((), ())), preferred_element_type=jnp.float32,
        )
        for k in (i, i + 1):
            for j in range(k, count):
                at = where[(k, j)] * block
                packed[at : at + block, :] = product[
                    (k - i) * block : (k - i + 1) * block, (j - i) * block : (j - i + 1) * block
                ]


def greet(devices):
    barrier = pltpu.get_barrier_semaphore()
    for device in devices:
        pl.semaphore_signal(
            barrier, inc=1, device_id=device, device_id_type=pl.DeviceIdType.MESH
        )
    pl.semaphore_wait(barrier, len(devices))


def remote(source, target, send, recv, device):
    copy = pltpu.make_async_remote_copy(
        src_ref=source, dst_ref=target, send_sem=send, recv_sem=recv,
        device_id=device, device_id_type=pl.DeviceIdType.MESH,
    )
    copy.start()
    return copy


def sum_kernel(
    leaves, fronts, block, order, assign, pattern, blocks, out,
    rows, far_rows, own_rows, far, own, landed, swapped, full,
    far_send, far_recv, own_send, own_recv, kept, send, recv, swap_send, swap_recv, send_back, recv_back,
):
    leaf, me = lax.axis_index("leaf"), lax.axis_index("front")
    team = leaves // 2
    side, mate = leaf // team, lax.rem(leaf, team)
    here, there = side * team, (1 - side) * team
    depth = far_rows.shape[0] // team
    strides = [2**level for level in range(fronts.bit_length() - 1)]
    sides = [lax.rem(me // stride, 2) for stride in strides]
    peers = [me + stride - 2 * stride * turn for stride, turn in zip(strides, sides)]
    levels = len(strides)
    half = far.shape[0] // 2
    orders = [list(range(levels)), list(reversed(range(levels)))]
    mates = [lax.rem(mate + d, team) for d in range(1, team)]
    opposite = there + mate
    greet([(here + other, me) for other in mates] + [(opposite, me)] + [(leaf, peer) for peer in peers])

    def at(start, size):
        return pl.ds(pl.multiple_of(start, SUB), size)

    def gather(base, target, send, recv, slot):
        place = target.at[at(mate * depth, depth)]
        copies = []
        for d, other in enumerate(mates):
            route_slot(order, assign, pattern, blocks, rows, base + other)
            copies.append(remote(
                rows.at[at((base + other) * depth, depth)], place, send.at[d], recv.at[d], (here + other, me)
            ))
        route_slot(order, assign, pattern, blocks, rows, base + mate)
        stay = pltpu.make_async_copy(rows.at[at((base + mate) * depth, depth)], place, kept.at[slot])
        stay.start()
        return copies + [stay]

    def scatter(part, which):
        offset = [0, half]
        size = half
        for level in range(levels):
            size = size // 2
            copies = []
            for way in range(2):
                axis = orders[way][level]
                keep = offset[way] + sides[axis] * size
                slot = (which * 2 + way) * levels + level
                place = way * half + half - 2 * size
                copies.append((
                    remote(
                        part.at[at(offset[way] + (1 - sides[axis]) * size, size)],
                        landed.at[which, pl.ds(place, size)],
                        send.at[slot], recv.at[slot], (leaf, peers[axis]),
                    ),
                    place,
                ))
                offset[way] = keep
            for way, (copy, place) in enumerate(copies):
                copy.wait()
                mine = at(offset[way], size)
                part[mine, :] = part[mine, :] + landed[which, place : place + size, :]
        return offset, size

    far_copies = gather(there, far_rows, far_send, far_recv, 0)
    own_copies = gather(here, own_rows, own_send, own_recv, 1)
    for copy in far_copies:
        copy.wait()
    gram_tiles(block, far_rows, far)
    offset, size = scatter(far, 0)
    swaps = [
        remote(
            far.at[at(offset[way], size)], swapped.at[pl.ds(way * size, size)],
            swap_send.at[way], swap_recv.at[way], (opposite, me),
        )
        for way in range(2)
    ]
    for copy in own_copies:
        copy.wait()
    gram_tiles(block, own_rows, own)
    offset, size = scatter(own, 1)
    for way, copy in enumerate(swaps):
        copy.wait()
        mine = at(offset[way], size)
        full[mine, :] = own[mine, :] + swapped[way * size : (way + 1) * size, :]
    for level in reversed(range(levels)):
        copies = []
        for way in range(2):
            axis = orders[way][level]
            slot = way * levels + level
            mine = full.at[at(offset[way], size)]
            copies.append(
                remote(mine, mine, send_back.at[slot], recv_back.at[slot], (leaf, peers[axis]))
            )
            offset[way] = offset[way] - sides[axis] * size
        for copy in copies:
            copy.wait()
        size = size * 2
    out[...] = full[...]


def route_slot(order, assign, pattern, blocks, rows, slot):
    count, size, width = blocks.shape
    column_blocks = pattern.shape[1]
    block = width // column_blocks
    found = [jnp.int32(count)] * CAP
    for b in range(count):
        free = assign[b] == order[slot]
        for p in range(CAP):
            take = jnp.logical_and(free, found[p] == count)
            found[p] = jnp.where(take, b, found[p])
            free = jnp.logical_and(free, jnp.logical_not(take))
    for p in range(CAP):
        source = jnp.minimum(found[p], count - 1)
        place = pl.ds(pl.multiple_of((slot * CAP + p) * size, size), size)
        for c in range(column_blocks):
            keep = jnp.where(found[p] < count, pattern[source, c], 0)
            cols = slice(c * block, (c + 1) * block)
            scale = jnp.full((size, block), keep, jnp.int32).astype(jnp.float32)
            rows[place, cols] = blocks[source, :, cols] * scale.astype(rows.dtype)


def swap_kernel(fronts, stride, own, out, got, send, recv, send_on, recv_on):
    leaf, me = lax.axis_index("leaf"), lax.axis_index("front")
    other = leaf + stride - 2 * stride * lax.rem(leaf // stride, 2)
    peers = [lax.rem(me + d, fronts) for d in range(1, fronts)]
    piece = own.shape[0] // fronts
    mine = pl.ds(pl.multiple_of(me * piece, SUB), piece)
    greet([(other, me)] + [(leaf, peer) for peer in peers])
    remote(own.at[mine], got.at[mine], send, recv, (other, me)).wait()
    copies = [
        remote(got.at[mine], got.at[mine], send_on.at[d], recv_on.at[d], (leaf, peer))
        for d, peer in enumerate(peers)
    ]
    for copy in copies:
        copy.wait()
    out[...] = got[...]


SMEM = pl.BlockSpec(memory_space=pltpu.SMEM)
VMEM = pl.BlockSpec(memory_space=pltpu.VMEM)


def gathered_gram(order, assign, pattern, blocks, leaves, fronts):
    _, block, width = blocks.shape
    packed = (len(pairs(width // block)) * block, block)
    team = leaves // 2
    levels = fronts.bit_length() - 1
    depth = CAP * block
    half_rows = (team * depth, width)

    def many(count):
        return pltpu.SemaphoreType.DMA((count,))

    return pl.pallas_call(
        functools.partial(sum_kernel, leaves, fronts, block),
        out_shape=jax.ShapeDtypeStruct(packed, jnp.float32),
        in_specs=[SMEM, SMEM, SMEM, VMEM],
        out_specs=VMEM,
        scratch_shapes=[
            pltpu.VMEM((leaves * depth, width), blocks.dtype),
            pltpu.VMEM(half_rows, blocks.dtype),
            pltpu.VMEM(half_rows, blocks.dtype),
            pltpu.VMEM(packed, jnp.float32),
            pltpu.VMEM(packed, jnp.float32),
            pltpu.VMEM((2,) + packed, jnp.float32),
            pltpu.VMEM((packed[0] // fronts, block), jnp.float32),
            pltpu.VMEM(packed, jnp.float32),
            many(team - 1), many(team - 1), many(team - 1), many(team - 1), many(2),
            many(4 * levels), many(4 * levels), many(2), many(2),
            many(2 * levels), many(2 * levels),
        ],
        compiler_params=pltpu.CompilerParams(
            collective_id=0, has_side_effects=True, vmem_limit_bytes=56 * 2**20
        ),
        name="gathered_gram",
    )(order, assign.reshape(-1), pattern, blocks)


def swap_leaves(own, fronts, stride):
    many = pltpu.SemaphoreType.DMA((fronts - 1,))
    one = pltpu.SemaphoreType.DMA
    return pl.pallas_call(
        functools.partial(swap_kernel, fronts, stride),
        out_shape=jax.ShapeDtypeStruct(own.shape, own.dtype),
        in_specs=[VMEM],
        out_specs=VMEM,
        scratch_shapes=[pltpu.VMEM(own.shape, own.dtype), one, one, many, many],
        compiler_params=pltpu.CompilerParams(
            collective_id=1, has_side_effects=True, vmem_limit_bytes=48 * 2**20
        ),
        name="swap_leaves",
    )(own)


def triangle_shape(width, block, fronts):
    rows = len(pairs(width // 2 // block)) * block + max(2 * (width // block), SUB * fronts)
    return jax.ShapeDtypeStruct((rows, block), jnp.float32)


def leaf_level(gram, weights, rows, block, fronts):
    width = weights.shape[1]
    return pl.pallas_call(
        functools.partial(leaf_kernel, block),
        out_shape=(
            jax.ShapeDtypeStruct((rows, width), jnp.float32),
            triangle_shape(width, block, fronts),
        ),
        in_specs=[VMEM, VMEM],
        out_specs=(VMEM, VMEM),
        scratch_shapes=work(width, block),
        compiler_params=pltpu.CompilerParams(vmem_limit_bytes=48 * 2**20),
        name="leaf_front",
    )(gram, weights)


def merge_level(own, other, maps, rows, width, block, pivots, fronts, level, name):
    outs = [jax.ShapeDtypeStruct((rows, width), jnp.float32)]
    if pivots < width:
        outs.append(triangle_shape(width, block, fronts))
    return pl.pallas_call(
        functools.partial(merge_kernel, block, pivots, fronts, level),
        out_shape=tuple(outs),
        in_specs=[SMEM, VMEM, VMEM],
        out_specs=tuple([VMEM] * len(outs)),
        scratch_shapes=work(width, block),
        compiler_params=pltpu.CompilerParams(vmem_limit_bytes=48 * 2**20),
        name=name,
    )(maps, own, other)


def local(blocks, pattern, assign, order, leaf_map, mid_map, prior):
    leaves = lax.axis_size("leaf")
    fronts = lax.axis_size("front")
    block_size, full_width = blocks.shape[1:]
    half_width = full_width // 2
    piece_rows = full_width // 4 // fronts
    gram = gathered_gram(order, assign, pattern, blocks, leaves, fronts)
    leaf_out, rest = leaf_level(gram, prior[0], half_width // fronts, block_size, fronts)
    mid_out, mid_rest = merge_level(
        rest, partner(rest, "leaf", 0), leaf_map, piece_rows, full_width, block_size, half_width, fronts, 1, "mid_front"
    )
    (top_out,) = merge_level(
        mid_rest, swap_leaves(mid_rest, fronts, 2), mid_map, piece_rows, full_width, block_size, full_width, fronts, 2,
        "top_front",
    )
    return (leaf_out[None], mid_out[None], top_out[None])


def solution(mesh):
    placed = (
        P(("leaf", "front"), None, None),
        P(("leaf", "front"), None),
        P(("leaf", "front"), None),
        P(),
        P(),
        P(),
        P("leaf", None, None),
    )
    return jax.shard_map(
        local,
        mesh=mesh,
        in_specs=placed,
        out_specs=(P("leaf", "front", None), P("leaf", "front", None), P("leaf", "front", None)),
        check_vma=False,
    )
```

```python
import functools
import jax
import jax.numpy as jnp
from jax import lax
from jax.experimental import pallas as pl
from jax.experimental.pallas import tpu as pltpu
from jax.sharding import PartitionSpec as P

CAP = 2
SUB = 8
NEAR = 3
HIGHEST = lax.Precision.HIGHEST


def partner(value, axis, stride):
    mask = 2**stride
    pairs = [(source, source ^ mask) for source in range(lax.axis_size(axis))]
    return lax.ppermute(value, axis, pairs)


def lanes(tile, column):
    return jnp.broadcast_to(tile[:, column : column + 1], tile.shape)


def subs(tile, row):
    return jnp.broadcast_to(tile[row : row + 1, :], tile.shape)


def factor_tile(diagonal):
    size = diagonal.shape[0]
    tiles = size // SUB
    shape = (SUB, size)
    sub_ids = lax.broadcasted_iota(jnp.int32, shape, 0)
    lane_ids = lax.broadcasted_iota(jnp.int32, shape, 1)
    picks = [sub_ids == p for p in range(SUB)]
    left = [diagonal[SUB * t : SUB * (t + 1), :] for t in range(tiles)]
    right = [(lane_ids == sub_ids + SUB * t).astype(jnp.float32) for t in range(tiles)]
    zero = left[0] * 0.0
    upper, inverse = [], []

    def columns_of(t, step):
        return [lanes(left[t], SUB * step + j) for j in range(SUB)]

    own = [column + zero for column in columns_of(0, 0)]
    for step in range(tiles):
        own_left, own_right = left[step], right[step]
        row_left, row_right = own_left, own_right
        near = range(step + 1, min(step + 1 + NEAR, tiles))
        ahead = {t: columns_of(t, step) for t in near}
        following = None
        if step + 1 < tiles:
            following = [column + zero for column in columns_of(step + 1, step + 1)]
        for p in range(SUB):
            scale = lax.rsqrt(subs(own[p], p))
            squared = scale * scale
            ratio = [None] * SUB
            for k in range(p + 1, SUB):
                row = subs(own[k], p)
                ratio[k] = row * squared
                if k == p + 1:
                    own[k] = own[k] - (own[p] * row) * squared
                else:
                    own[k] = own[k] - own[p] * ratio[k]
            pivot_left, pivot_right = subs(own_left, p), subs(own_right, p)
            row_left = jnp.where(picks[p], pivot_left * scale, row_left)
            row_right = jnp.where(picks[p], pivot_right * scale, row_right)
            pivot_left, pivot_right = pivot_left * squared, pivot_right * squared
            if p < SUB - 1:
                own_left = own_left - own[p] * pivot_left
                own_right = own_right - own[p] * pivot_right
            if following is not None:
                scaled = ahead[step + 1][p] * squared
                for k in range(SUB):
                    following[k] = following[k] - ahead[step + 1][p] * subs(scaled, k)
            for t in near:
                left[t] = left[t] - ahead[t][p] * pivot_left
                right[t] = right[t] - ahead[t][p] * pivot_right
                for k in range(p + 1, SUB):
                    ahead[t][k] = ahead[t][k] - ahead[t][p] * ratio[k]
        upper.append(row_left)
        inverse.append(row_right)
        own = following
        if step + 1 + NEAR < tiles:
            high, low = halves(jnp.concatenate([row_left, row_right], 1))
            change = product((high[:, :size], low[:, :size]), (high, low), 0)
            for t in range(step + 1 + NEAR, tiles):
                rows = slice(SUB * t, SUB * (t + 1))
                left[t] = left[t] - change[rows, :size]
                right[t] = right[t] - change[rows, size:]
    return jnp.concatenate(upper, 0), jnp.concatenate(inverse, 0)


def halves(value):
    high = value.astype(jnp.bfloat16)
    return high, (value - high.astype(jnp.float32)).astype(jnp.bfloat16)


def stacked(left, right, contract):
    return (
        jnp.concatenate([left[0], left[0], left[1]], contract),
        jnp.concatenate([right[0], right[1], right[0]], 0),
    )


def dot(left, right, contract):
    return lax.dot_general(
        left, right, (((contract,), (0,)), ((), ())), preferred_element_type=jnp.float32
    )


def product(left, right, contract):
    return dot(*stacked(left, right, contract), contract)


def eliminate(front, diagonal, over, under, pivots, block, touched=None):
    width = front.shape[0]
    blocks = width // block
    shape = (block, block)
    same = lax.broadcasted_iota(jnp.int32, shape, 0) == lax.broadcasted_iota(jnp.int32, shape, 1)
    lane_ids = lax.broadcasted_iota(jnp.int32, (block, width), 1)

    def put_off(first):
        start = first
        while start < blocks:
            stop = min(start + 2, blocks)
            rows = slice(start * block, stop * block)
            front[rows, start * block :] = front[rows, start * block :] - dot(
                over[:, rows], under[:, start * block :], 0
            )
            start = stop

    def step(first, index, carry):
        start = pl.multiple_of(index * block, block)
        rows = pl.ds(start, block)
        after = pl.ds(pl.multiple_of(jnp.minimum(index + 1, blocks - 1) * block, block), block)

        def dense():
            upper, inverse = factor_tile(diagonal[...])
            put_off(first)
            row = product(halves(inverse), halves(front[rows, :]), 1)
            front[rows, :] = row
            front[rows, rows] = upper
            parts = halves(jnp.where(lane_ids >= start + block, row, 0.0))
            over[...], under[...] = stacked(parts, parts, 0)
            diagonal[...] = front[after, after] - dot(over[:, after], under[:, after], 0)

        if touched is None:
            dense()
        else:
            here = touched(index)
            pl.when(here)(dense)

            @pl.when(jnp.logical_not(here))
            def _():
                put_off(first)
                tile = front[rows, rows]
                front[rows, rows] = jnp.where(same, tile * lax.rsqrt(tile), 0.0)
                over[...] = jnp.zeros_like(over)
                under[...] = jnp.zeros_like(under)
                diagonal[...] = front[after, after]

        return carry

    over[...] = jnp.zeros_like(over)
    under[...] = jnp.zeros_like(under)
    diagonal[...] = front[:block, :block]
    panels = pivots // block
    middle = min(panels, blocks // 2)
    lax.fori_loop(0, middle, functools.partial(step, 1), 0)
    if middle < panels:
        lax.fori_loop(middle, panels, functools.partial(step, middle), 0)
    put_off(panels)


def work(width, block):
    return [
        pltpu.VMEM((width, width), jnp.float32),
        pltpu.VMEM((block, block), jnp.float32),
        pltpu.VMEM((3 * block, width), jnp.bfloat16),
        pltpu.VMEM((3 * block, width), jnp.bfloat16),
    ]


def add_weights(front, weight_of, block):
    size = front.shape[0]
    same = lax.broadcasted_iota(jnp.int32, (block, block), 0) == lax.broadcasted_iota(
        jnp.int32, (block, block), 1
    )
    for start in range(0, size, block):
        at = slice(start, start + block)
        front[at, at] = front[at, at] + jnp.where(same, weight_of(start // block), 0.0)


def take_rows(front, out, start):
    count, width = out.shape
    row_ids = start + lax.broadcasted_iota(jnp.int32, (count, width), 0)
    lane_ids = lax.broadcasted_iota(jnp.int32, (count, width), 1)
    out[...] = jnp.where(lane_ids >= row_ids, front[pl.ds(start, count), :], 0.0)


def pairs(count):
    return [(i, j) for i in range(count) for j in range(i, count)]


def pack_triangle(front, packed, first, block):
    count = front.shape[0] // block - first
    for index, (i, j) in enumerate(pairs(count)):
        rows, cols = (first + i) * block, (first + j) * block
        packed[index * block : (index + 1) * block, :] = front[
            rows : rows + block, cols : cols + block
        ]


def carry_rows(packed, base, rows):
    packed[base:, :] = jnp.zeros((packed.shape[0] - base, packed.shape[1]), packed.dtype)
    for index, row in enumerate(rows):
        packed[base + index : base + index + 1, :] = row


def leaf_kernel(block, gram, weights, out, rest, front, diagonal, over, under):
    width = front.shape[0]
    blocks = width // block
    for index, (i, j) in enumerate(pairs(blocks)):
        front[i * block : (i + 1) * block, j * block : (j + 1) * block] = gram[
            index * block : (index + 1) * block, :
        ]

    def weight_of(level, b):
        return weights[level : level + 1, b * block : (b + 1) * block]

    add_weights(front, functools.partial(weight_of, 0), block)
    base = len(pairs(blocks // 2)) * block
    carry_rows(rest, base, [weight_of(level, b) for level in (1, 2) for b in range(blocks)])
    eliminate(front, diagonal, over, under, width // 2, block)
    take_rows(front, out, pl.multiple_of(lax.axis_index("front") * out.shape[0], SUB))
    pack_triangle(front, rest, blocks // 2, block)


def merge_kernel(block, pivots, fronts, level, maps, own, other, out, *more):
    *more, front, diagonal, over, under = more
    width = front.shape[0]
    half = width // 2
    blocks = width // block
    base = len(pairs(blocks // 2)) * block
    leaf = lax.axis_index("leaf")
    below = 2 ** (level - 1)
    mine = leaf // below
    theirs = mine + 1 - 2 * lax.rem(mine, 2)
    front[...] = jnp.zeros_like(front)
    add_weights(front, lambda b: own[base + b : base + b + 1, :] + other[base + b : base + b + 1, :], block)
    for source, child in ((mine, own), (theirs, other)):
        for index, (i, j) in enumerate(pairs(half // block)):
            tile = child[index * block : (index + 1) * block, :]
            row, column = maps[source, i], maps[source, j]
            first = pl.ds(pl.multiple_of(row * block, block), block)
            second = pl.ds(pl.multiple_of(column * block, block), block)

            def plain(first=first, second=second, tile=tile):
                front[first, second] = front[first, second] + tile

            def turned(first=first, second=second, tile=tile):
                front[second, first] = front[second, first] + tile.T

            if i == j:
                plain()
            else:
                pl.when(row < column)(plain)
                pl.when(row > column)(turned)

    def touched(index):
        found = maps[mine, 0] == index
        for source in (mine, theirs):
            for i in range(half // block):
                found = jnp.logical_or(found, maps[source, i] == index)
        return found

    eliminate(front, diagonal, over, under, pivots, block, touched)
    turn = lax.rem(leaf, 2**level) * fronts + lax.axis_index("front")
    take_rows(front, out, pl.multiple_of(turn * out.shape[0], SUB))
    if more:
        carry_rows(more[0], base, [
            own[base + b : base + b + 1, :] + other[base + b : base + b + 1, :]
            for b in range(blocks, 2 * blocks)
        ])
        pack_triangle(front, more[0], half // block, block)


def gram_tiles(block, rows, packed):
    width = rows.shape[1]
    count = width // block
    where = {pair: index for index, pair in enumerate(pairs(count))}
    for i in range(0, count, 2):
        product = lax.dot_general(
            rows[:, i * block : (i + 2) * block], rows[:, i * block :],
            (((0,), (0,)), ((), ())), preferred_element_type=jnp.float32,
        )
        for k in (i, i + 1):
            for j in range(k, count):
                at = where[(k, j)] * block
                packed[at : at + block, :] = product[
                    (k - i) * block : (k - i + 1) * block, (j - i) * block : (j - i + 1) * block
                ]


def greet(devices):
    barrier = pltpu.get_barrier_semaphore()
    for device in devices:
        pl.semaphore_signal(
            barrier, inc=1, device_id=device, device_id_type=pl.DeviceIdType.MESH
        )
    pl.semaphore_wait(barrier, len(devices))


def remote(source, target, send, recv, device):
    copy = pltpu.make_async_remote_copy(
        src_ref=source, dst_ref=target, send_sem=send, recv_sem=recv,
        device_id=device, device_id_type=pl.DeviceIdType.MESH,
    )
    copy.start()
    return copy


def sum_kernel(
    leaves, fronts, block, order, assign, pattern, blocks, out,
    rows, far_rows, own_rows, far, own, landed, swapped, full,
    far_send, far_recv, own_send, own_recv, kept, send, recv, swap_send, swap_recv, send_back, recv_back,
):
    leaf, me = lax.axis_index("leaf"), lax.axis_index("front")
    team = leaves // 2
    side, mate = leaf // team, lax.rem(leaf, team)
    here, there = side * team, (1 - side) * team
    depth = far_rows.shape[0] // team
    strides = [2**level for level in range(fronts.bit_length() - 1)]
    sides = [lax.rem(me // stride, 2) for stride in strides]
    peers = [me + stride - 2 * stride * turn for stride, turn in zip(strides, sides)]
    levels = len(strides)
    half = far.shape[0] // 2
    orders = [list(range(levels)), list(reversed(range(levels)))]
    mates = [lax.rem(mate + d, team) for d in range(1, team)]
    opposite = there + mate
    greet([(here + other, me) for other in mates] + [(opposite, me)] + [(leaf, peer) for peer in peers])

    def at(start, size):
        return pl.ds(pl.multiple_of(start, SUB), size)

    def gather(base, target, send, recv, slot):
        place = target.at[at(mate * depth, depth)]
        copies = []
        for d, other in enumerate(mates):
            route_slot(order, assign, pattern, blocks, rows, base + other)
            copies.append(remote(
                rows.at[at((base + other) * depth, depth)], place, send.at[d], recv.at[d], (here + other, me)
            ))
        route_slot(order, assign, pattern, blocks, rows, base + mate)
        stay = pltpu.make_async_copy(rows.at[at((base + mate) * depth, depth)], place, kept.at[slot])
        stay.start()
        return copies + [stay]

    def scatter(part, which):
        offset = [0, half]
        size = half
        for level in range(levels):
            size = size // 2
            copies = []
            for way in range(2):
                axis = orders[way][level]
                keep = offset[way] + sides[axis] * size
                slot = (which * 2 + way) * levels + level
                place = way * half + half - 2 * size
                copies.append((
                    remote(
                        part.at[at(offset[way] + (1 - sides[axis]) * size, size)],
                        landed.at[which, pl.ds(place, size)],
                        send.at[slot], recv.at[slot], (leaf, peers[axis]),
                    ),
                    place,
                ))
                offset[way] = keep
            for way, (copy, place) in enumerate(copies):
                copy.wait()
                mine = at(offset[way], size)
                part[mine, :] = part[mine, :] + landed[which, place : place + size, :]
        return offset, size

    far_copies = gather(there, far_rows, far_send, far_recv, 0)
    own_copies = gather(here, own_rows, own_send, own_recv, 1)
    for copy in far_copies:
        copy.wait()
    gram_tiles(block, far_rows, far)
    offset, size = scatter(far, 0)
    swaps = [
        remote(
            far.at[at(offset[way], size)], swapped.at[pl.ds(way * size, size)],
            swap_send.at[way], swap_recv.at[way], (opposite, me),
        )
        for way in range(2)
    ]
    for copy in own_copies:
        copy.wait()
    gram_tiles(block, own_rows, own)
    offset, size = scatter(own, 1)
    for way, copy in enumerate(swaps):
        copy.wait()
        mine = at(offset[way], size)
        full[mine, :] = own[mine, :] + swapped[way * size : (way + 1) * size, :]
    for level in reversed(range(levels)):
        copies = []
        for way in range(2):
            axis = orders[way][level]
            slot = way * levels + level
            mine = full.at[at(offset[way], size)]
            copies.append(
                remote(mine, mine, send_back.at[slot], recv_back.at[slot], (leaf, peers[axis]))
            )
            offset[way] = offset[way] - sides[axis] * size
        for copy in copies:
            copy.wait()
        size = size * 2
    out[...] = full[...]


def route_slot(order, assign, pattern, blocks, rows, slot):
    count, size, width = blocks.shape
    column_blocks = pattern.shape[1]
    block = width // column_blocks
    found = [jnp.int32(count)] * CAP
    for b in range(count):
        free = assign[b] == order[slot]
        for p in range(CAP):
            take = jnp.logical_and(free, found[p] == count)
            found[p] = jnp.where(take, b, found[p])
            free = jnp.logical_and(free, jnp.logical_not(take))
    for p in range(CAP):
        source = jnp.minimum(found[p], count - 1)
        place = pl.ds(pl.multiple_of((slot * CAP + p) * size, size), size)
        for c in range(column_blocks):
            keep = jnp.where(found[p] < count, pattern[source, c], 0)
            cols = slice(c * block, (c + 1) * block)
            scale = jnp.full((size, block), keep, jnp.int32).astype(jnp.float32)
            rows[place, cols] = blocks[source, :, cols] * scale.astype(rows.dtype)


def swap_kernel(fronts, stride, own, out, got, send, recv, send_on, recv_on):
    leaf, me = lax.axis_index("leaf"), lax.axis_index("front")
    other = leaf + stride - 2 * stride * lax.rem(leaf // stride, 2)
    peers = [lax.rem(me + d, fronts) for d in range(1, fronts)]
    piece = own.shape[0] // fronts
    mine = pl.ds(pl.multiple_of(me * piece, SUB), piece)
    greet([(other, me)] + [(leaf, peer) for peer in peers])
    remote(own.at[mine], got.at[mine], send, recv, (other, me)).wait()
    copies = [
        remote(got.at[mine], got.at[mine], send_on.at[d], recv_on.at[d], (leaf, peer))
        for d, peer in enumerate(peers)
    ]
    for copy in copies:
        copy.wait()
    out[...] = got[...]


SMEM = pl.BlockSpec(memory_space=pltpu.SMEM)
VMEM = pl.BlockSpec(memory_space=pltpu.VMEM)


def gathered_gram(order, assign, pattern, blocks, leaves, fronts):
    _, block, width = blocks.shape
    packed = (len(pairs(width // block)) * block, block)
    team = leaves // 2
    levels = fronts.bit_length() - 1
    depth = CAP * block
    half_rows = (team * depth, width)

    def many(count):
        return pltpu.SemaphoreType.DMA((count,))

    return pl.pallas_call(
        functools.partial(sum_kernel, leaves, fronts, block),
        out_shape=jax.ShapeDtypeStruct(packed, jnp.float32),
        in_specs=[SMEM, SMEM, SMEM, VMEM],
        out_specs=VMEM,
        scratch_shapes=[
            pltpu.VMEM((leaves * depth, width), blocks.dtype),
            pltpu.VMEM(half_rows, blocks.dtype),
            pltpu.VMEM(half_rows, blocks.dtype),
            pltpu.VMEM(packed, jnp.float32),
            pltpu.VMEM(packed, jnp.float32),
            pltpu.VMEM((2,) + packed, jnp.float32),
            pltpu.VMEM((packed[0] // fronts, block), jnp.float32),
            pltpu.VMEM(packed, jnp.float32),
            many(team - 1), many(team - 1), many(team - 1), many(team - 1), many(2),
            many(4 * levels), many(4 * levels), many(2), many(2),
            many(2 * levels), many(2 * levels),
        ],
        compiler_params=pltpu.CompilerParams(
            collective_id=0, has_side_effects=True, vmem_limit_bytes=40 * 2**20
        ),
        name="gathered_gram",
    )(order, assign.reshape(-1), pattern, blocks)


def swap_leaves(own, fronts, stride):
    many = pltpu.SemaphoreType.DMA((fronts - 1,))
    one = pltpu.SemaphoreType.DMA
    return pl.pallas_call(
        functools.partial(swap_kernel, fronts, stride),
        out_shape=jax.ShapeDtypeStruct(own.shape, own.dtype),
        in_specs=[VMEM],
        out_specs=VMEM,
        scratch_shapes=[pltpu.VMEM(own.shape, own.dtype), one, one, many, many],
        compiler_params=pltpu.CompilerParams(
            collective_id=1, has_side_effects=True, vmem_limit_bytes=48 * 2**20
        ),
        name="swap_leaves",
    )(own)


def triangle_shape(width, block, fronts):
    rows = len(pairs(width // 2 // block)) * block + max(2 * (width // block), SUB * fronts)
    return jax.ShapeDtypeStruct((rows, block), jnp.float32)


def leaf_level(gram, weights, rows, block, fronts):
    width = weights.shape[1]
    return pl.pallas_call(
        functools.partial(leaf_kernel, block),
        out_shape=(
            jax.ShapeDtypeStruct((rows, width), jnp.float32),
            triangle_shape(width, block, fronts),
        ),
        in_specs=[VMEM, VMEM],
        out_specs=(VMEM, VMEM),
        scratch_shapes=work(width, block),
        compiler_params=pltpu.CompilerParams(vmem_limit_bytes=48 * 2**20),
        name="leaf_front",
    )(gram, weights)


def merge_level(own, other, maps, rows, width, block, pivots, fronts, level, name):
    outs = [jax.ShapeDtypeStruct((rows, width), jnp.float32)]
    if pivots < width:
        outs.append(triangle_shape(width, block, fronts))
    return pl.pallas_call(
        functools.partial(merge_kernel, block, pivots, fronts, level),
        out_shape=tuple(outs),
        in_specs=[SMEM, VMEM, VMEM],
        out_specs=tuple([VMEM] * len(outs)),
        scratch_shapes=work(width, block),
        compiler_params=pltpu.CompilerParams(vmem_limit_bytes=48 * 2**20),
        name=name,
    )(maps, own, other)


def local(blocks, pattern, assign, order, leaf_map, mid_map, prior):
    leaves = lax.axis_size("leaf")
    fronts = lax.axis_size("front")
    block_size, full_width = blocks.shape[1:]
    half_width = full_width // 2
    piece_rows = full_width // 4 // fronts
    gram = gathered_gram(order, assign, pattern, blocks, leaves, fronts)
    leaf_out, rest = leaf_level(gram, prior[0], half_width // fronts, block_size, fronts)
    mid_out, mid_rest = merge_level(
        rest, partner(rest, "leaf", 0), leaf_map, piece_rows, full_width, block_size, half_width, fronts, 1, "mid_front"
    )
    (top_out,) = merge_level(
        mid_rest, swap_leaves(mid_rest, fronts, 2), mid_map, piece_rows, full_width, block_size, full_width, fronts, 2,
        "top_front",
    )
    return (leaf_out[None], mid_out[None], top_out[None])


def solution(mesh):
    placed = (
        P(("leaf", "front"), None, None),
        P(("leaf", "front"), None),
        P(("leaf", "front"), None),
        P(),
        P(),
        P(),
        P("leaf", None, None),
    )
    return jax.shard_map(
        local,
        mesh=mesh,
        in_specs=placed,
        out_specs=(P("leaf", "front", None), P("leaf", "front", None), P("leaf", "front", None)),
        check_vma=False,
    )
```
